256 devices in a mesh: dp: 8 (over y, z_lo), fsdp: 32 (over z_hi, x, core).
Axes of the slice: x: 4, y: 4, z: 8 (z_hi: 4, z_lo: 2; z = z_hi * 2 + z_lo), core: 2. Of those that a mesh axis runs over, the one named last changes fastest.
Arguments:
- acts: bfloat16 [114688, 7168], P(('dp', 'fsdp')), may hold values from -24 to 24
- upstream: bfloat16 [114688, 512], P(('dp', 'fsdp')), may hold values from -0.4375 to 0.4375
- k_weight: bfloat16 [7168, 512], P('fsdp'), may hold values from -0.0625 to 0.0625
- probe: bfloat16 [7168, 512], P('fsdp'), may hold values from -5 to 5
- norm_gain: float32 [128], replicated, may hold values from 0.1 to 1.9
- momentum: float32 [7168, 512], P('fsdp', 'dp'), may hold values from -4 to 4
- curvature: float32 [7168, 512], P('fsdp', 'dp'), may hold values from 0.3 to 3
Outputs:
- new_momentum: float32 [7168, 512], P('fsdp', 'dp')
- new_curvature: float32 [7168, 512], P('fsdp', 'dp')
- update: float32 [7168, 512], P('fsdp', 'dp')
The draws below stay inside these ranges and needn't reach their ends.
All inputs are finite; a program needn't handle non-finite values.
Results may differ from the reference program's by a relative error of at most 0.024.
Values may be sent and summed in bfloat16 or wider, within the bound.
A program may use at most 128 MiB of HBM per device.

```python
import math
import jax
import jax.numpy as jnp
from jax import lax

D = 7168
HEAD_DIM = 128
TOK_DEV = 448
KV_WIDTH = 512
TOKENS = 114688


def strengthened(drawn, rng, source, target, blocks, factor):
    def block_of(position):
        return (jnp.arange(drawn.shape[position]) // (drawn.shape[position] // blocks)).reshape((-1,) + (1,) * (drawn.ndim - 1 - position))

    one_side = jax.random.permutation(rng, blocks)[block_of(target)]
    far = (block_of(target) + blocks // 2) % blocks
    return jnp.where((block_of(source) == one_side) | (block_of(source) == far), factor * drawn, drawn)


def block_levels(stream_key, extent, split, smallest, top_value):
    gain = 1.0
    for dim, shards_of in split:
        draws = jax.random.uniform(jax.random.fold_in(jax.random.fold_in(stream_key, 6), dim), (shards_of,), jnp.float32, smallest / len(split), top_value / len(split))
        gain = gain * jnp.repeat(jnp.exp(draws), extent[dim] // shards_of).reshape((-1,) + (1,) * (len(extent) - 1 - dim))
    return gain


def gaussian(stream_key, shape, deviation, bound, cuts=(), held_as=jnp.bfloat16):
    factor_of = block_levels(stream_key, shape, cuts, -0.22, 0.18) if cuts else 1.0
    result = jax.random.normal(stream_key, shape, jnp.float32) * deviation * factor_of
    return jnp.minimum(jnp.maximum(result, -bound), bound).astype(held_as)


def gaussian_with(own_key, dims, scale, reach, split, heavy, held_as=jnp.bfloat16):
    result = scale * jax.random.normal(own_key, dims, jnp.float32)
    if split:
        result = result * block_levels(own_key, dims, split, -0.22, 0.18)
    return jnp.clip(strengthened(result, jax.random.fold_in(own_key, 3), *heavy), -reach, reach).astype(held_as)


def setup_inputs(seed: int = 0) -> dict:
    splits = jax.random.split(jax.random.key(seed), 8)
    acts = gaussian_with(splits[0], (TOKENS, D), 1.0, 24.0, ((0, 256),), (0, 1, 256, 6.0))
    upstream = gaussian(splits[1], (TOKENS, KV_WIDTH), (10 * TOKENS ** -0.5), 0.4375, ((0, 256),))
    k_weight = gaussian(splits[2], (D, KV_WIDTH), D ** -0.5, 0.0625, ((0, 32),))
    probe = gaussian(splits[3], (D, KV_WIDTH), 1.0, 5.0, ((0, 32),))
    norm_gain = jnp.clip(1.0 + 0.18 * jax.random.normal(splits[4], (HEAD_DIM,), jnp.float32), 0.1, 1.9)
    momentum = gaussian(splits[5], (D, KV_WIDTH), 0.3, 4.0, ((0, 32), (1, 8)), jnp.float32)
    curvature = jnp.clip(jnp.exp(math.log(3.0) - 2.3025851 * jax.random.uniform(splits[6], (D, KV_WIDTH), jnp.float32) ** block_levels(splits[6], (D, KV_WIDTH), ((0, 32), (1, 8)), -0.2, 0.2)), 0.3, 3.0)
    return {"acts": acts, "upstream": upstream, "k_weight": k_weight, "probe": probe, "norm_gain": norm_gain, "momentum": momentum, "curvature": curvature}


def head_terms(projected, tangent, upstream, norm_gain):
    token_count = projected.shape[0]
    head_size = norm_gain.shape[0]
    head_count = projected.shape[1] // head_size
    shaped = (token_count, head_count, head_size)
    values = projected.reshape(shaped)
    moving = tangent.reshape(shaped)
    weighted = upstream.astype(jnp.float32).reshape(shaped) * norm_gain
    inverse = lax.rsqrt(lax.optimization_barrier(jnp.mean(values * values, axis=-1, keepdims=True)) + 1e-06)
    cubed = inverse * inverse * inverse
    along = lax.optimization_barrier(jnp.sum(weighted * values, axis=-1, keepdims=True))
    grad_vals = inverse * weighted - cubed * values * along / head_size
    inverse_dot = -cubed * lax.optimization_barrier(jnp.sum(values * moving, axis=-1, keepdims=True)) / head_size
    along_dot = lax.optimization_barrier(jnp.sum(weighted * moving, axis=-1, keepdims=True))
    hvp_vals = inverse_dot * weighted - (3.0 * inverse * inverse * inverse_dot * values * along + cubed * moving * along + cubed * values * along_dot) / head_size
    return (grad_vals.reshape(token_count, -1), hvp_vals.reshape(token_count, -1))

def reference(acts, upstream, k_weight, probe, norm_gain, momentum, curvature):
    width = k_weight.shape[1]
    model_width = acts.shape[1]

    def block_step(carry, pieces):
        act_rows, cot_rows = pieces
        projected = jnp.dot(act_rows, k_weight, preferred_element_type=jnp.float32)
        tangent = jnp.dot(act_rows, probe, preferred_element_type=jnp.float32)
        grad_vals, hvp_vals = head_terms(projected, tangent, cot_rows, norm_gain)
        stacked = jnp.concatenate([grad_vals, hvp_vals], axis=1).astype(jnp.bfloat16)
        partial_sum = lax.dot_general(act_rows, stacked, (((0,), (0,)), ((), ())), preferred_element_type=jnp.float32)
        rounded = lax.optimization_barrier(partial_sum.astype(jnp.bfloat16))
        return (carry + rounded.astype(jnp.float32), None)
    blocks = acts.reshape(-1, TOK_DEV, model_width)
    cot_blocks = upstream.reshape(-1, TOK_DEV, width)
    total, unused = lax.scan(block_step, jnp.zeros((model_width, 2 * width), jnp.float32), (blocks, cot_blocks))
    gradient = total[:, :width]
    hvp = total[:, width:]
    new_momentum = 0.965 * momentum + 0.035 * gradient
    new_curvature = 0.99 * curvature + 0.01 * (probe.astype(jnp.float32) * hvp)
    update = jnp.clip(new_momentum / jnp.maximum(0.5 * new_curvature, 0.25), -1.0, 1.0)
    return (new_momentum, new_curvature, update)
```

```python
import jax
import jax.numpy as jnp
from jax import lax
from jax.experimental import pallas as pl
from jax.experimental.pallas import tpu as pltpu
from jax.sharding import PartitionSpec as P

MESH = pl.DeviceIdType.MESH
F32 = jnp.float32
BF16 = jnp.bfloat16
TOK = 448
D = 7168
NX = 400


def kernel(acts, upstream, k_weight, probe, gain, momentum, curvature,
           out_m, out_c, out_u,
           wp, av, at, acc, upv, gs, csend, crecv, rsend, rech, recf, s_buf,
           yrecv, t_buf, zrecv, mom_v, cur_v, send_sems, recv_sems, loc_sems):
    dp = lax.axis_index("dp")
    fs = lax.axis_index("fsdp")
    y, zl = dp // 2, lax.rem(dp, 2)
    zh, x, c = fs // 8, lax.rem(fs // 2, 4), lax.rem(fs, 2)

    def m4(v):
        return lax.rem(v + 8, 4)

    def dev(dx=0, dy=0, dz=0):
        return (m4(y + dy) * 2 + zl, m4(zh + dz) * 8 + m4(x + dx) * 2 + c)

    def dev_z(z):
        return (y * 2 + lax.rem(z, 2), (z // 2) * 8 + x * 2 + c)

    partner = (dp, zh * 8 + x * 2 + (1 - c))
    z = 2 * zh + zl

    barrier = pltpu.get_barrier_semaphore()
    peers = [partner]
    for d in (1, 2, 3):
        peers += [dev(dx=d), dev(dy=d)]
    for d in range(1, 8):
        peers.append(dev_z(lax.rem(z + d, 8)))

    def local(src, dst, i):
        cp = pltpu.make_async_copy(src, dst, loc_sems.at[i])
        cp.start()
        return cp

    low_rows, high_rows = pl.ds(0, 112), pl.ds(112, 112)
    quarter = wp.at[zh, x, c, high_rows, pl.ds(pl.multiple_of(y * 256, 256), 256)]
    part_cols = pl.ds(pl.multiple_of(lax.rem(y, 2) * 256, 256), 256)

    @pl.when(y < 2)
    def _():
        pltpu.make_async_copy(k_weight.at[high_rows, part_cols], quarter, loc_sems.at[13]).start()

    @pl.when(y >= 2)
    def _():
        pltpu.make_async_copy(probe.at[high_rows, part_cols], quarter, loc_sems.at[13]).start()

    own = [local(k_weight.at[low_rows], wp.at[zh, x, c, low_rows, pl.ds(0, 512)], 0),
           local(probe.at[low_rows], wp.at[zh, x, c, low_rows, pl.ds(512, 512)], 1),
           pltpu.make_async_copy(k_weight.at[high_rows, part_cols], quarter, loc_sems.at[13])]
    acp = [local(acts.at[:, pl.ds(i * 896, 896)], av.at[:, pl.ds(i * 896, 896)], 2 + i) for i in range(8)]
    misc = [local(upstream, upv, 10), local(momentum, mom_v, 11), local(curvature, cur_v, 12)]

    for p in peers:
        pl.semaphore_signal(barrier, inc=1, device_id=p, device_id_type=MESH)
    pl.semaphore_wait(barrier, len(peers))

    count = [0]
    sent = []

    def take(n):
        base = count[0]
        count[0] += n
        return base

    def rdma(src, dst, device, i):
        return pltpu.make_async_remote_copy(
            src_ref=src, dst_ref=dst, send_sem=send_sems.at[i], recv_sem=recv_sems.at[i],
            device_id=device, device_id_type=MESH)

    def xfer(src, dst, device):
        cp = rdma(src, dst, device, take(1))
        cp.start()
        sent.append(cp)
        return cp

    class Ring:
        def __init__(self, region, half, coord, up, down):
            self.region, self.half, self.coord, self.up, self.down = region, half, coord, up, down

        def start(self):
            r = self.region(self.coord)
            self.p = xfer(r, r, self.up)
            self.m = xfer(r, r, self.down)

        def mid(self):
            self.p.wait_recv()
            r = self.half(m4(self.coord - 1), 0)
            self.hp = xfer(r, r, self.up)
            self.m.wait_recv()
            r = self.half(m4(self.coord + 1), 1)
            self.hm = xfer(r, r, self.down)

        def end(self):
            self.hp.wait_recv()
            self.hm.wait_recv()

    lo, hi = pl.ds(0, 112), pl.ds(112, 112)
    yc = pl.multiple_of(y * 256, 256)

    def bz_half(q, i):
        return wp.at[q, x, c, hi, pl.ds(pl.multiple_of(yc + i * 128, 128), 128)]

    bz = Ring(lambda q: wp.at[q, x, c, hi, pl.ds(yc, 256)], bz_half, zh, dev(dz=1), dev(dz=-1))
    az = Ring(lambda q: wp.at[q, x, c, lo, :],
              lambda q, i: wp.at[q, x, c, lo, pl.ds(i * 512, 512)], zh, dev(dz=1), dev(dz=-1))
    bx, ax, by = {}, {}, {}
    for dz in (0, -1, 1, 2):
        def mk(q):
            bx[dz] = Ring(lambda k: wp.at[q, k, c, hi, pl.ds(yc, 256)],
                          lambda k, i: wp.at[q, k, c, hi, pl.ds(pl.multiple_of(yc + i * 128, 128), 128)],
                          x, dev(dx=1), dev(dx=-1))
            ax[dz] = Ring(lambda k: wp.at[q, k, c, lo, :],
                          lambda k, i: wp.at[q, k, c, lo, pl.ds(i * 512, 512)],
                          x, dev(dx=1), dev(dx=-1))
            by[dz] = Ring(lambda k: wp.at[q, :, c, hi, pl.ds(pl.multiple_of(k * 256, 256), 256)],
                          lambda k, i: wp.at[q, pl.ds(2 * i, 2), c, hi, pl.ds(pl.multiple_of(k * 256, 256), 256)],
                          y, dev(dy=1), dev(dy=-1))
        mk(m4(zh + dz))

    core = {}

    def core_send(kind, dz):
        r = wp.at[m4(zh + dz), :, c, lo if kind == "a" else hi, :]
        core[kind, dz] = xfer(r, r, partner)

    def transpose(i):
        acp[i].wait()
        q, xp = i // 2, i % 2
        blk = av[:, i * 896:(i + 1) * 896]
        tr = blk.T
        for xx in range(2):
            for cc in range(2):
                for col in range(2):
                    r0 = xx * 448 + cc * 224 + col * 112
                    at[col, xp * 2 + xx, cc, pl.ds(q * 112, 112), :] = tr[r0:r0 + 112, :]

    first = [True]

    def forward(dz):
        core["a", dz].wait_recv()
        core["b", dz].wait_recv()
        q = m4(zh + dz)
        init = first[0]
        first[0] = False
        for n in range(2):
            total = None if init else acc[:, n * 512:(n + 1) * 512]
            for xp in range(2):
                lhs = av[:, pl.ds(pl.multiple_of(q * 1792 + xp * 896, 128), 896)]
                rhs = wp[q, xp * 2:xp * 2 + 2, :, :, n * 512:(n + 1) * 512].reshape(896, 512)
                part = jnp.dot(lhs, rhs, preferred_element_type=F32)
                total = part if total is None else total + part
            acc[:, n * 512:(n + 1) * 512] = total

    for cp in own:
        cp.wait()
    bz.start()
    bx[0].start()
    ax[0].start()
    transpose(0)
    bx[0].mid()
    bz.mid()
    az.start()
    bx[-1].start()
    bx[1].start()
    transpose(1)
    bx[0].end()
    by[0].start()
    transpose(2)
    bx[-1].mid()
    bx[1].mid()
    ax[0].mid()
    bz.end()
    bx[2].start()
    transpose(3)
    bx[-1].end()
    by[-1].start()
    bx[1].end()
    by[1].start()
    transpose(4)
    bx[2].mid()
    transpose(5)
    bx[2].end()
    by[2].start()
    by[0].mid()
    ax[0].end()
    core_send("a", 0)
    transpose(6)
    az.mid()
    ax[-1].start()
    ax[1].start()
    transpose(7)
    by[0].end()
    core_send("b", 0)
    by[-1].mid()
    forward(0)
    az.end()
    ax[2].start()
    by[-1].end()
    core_send("b", -1)
    ax[-1].mid()
    ax[1].mid()
    by[1].mid()
    ax[-1].end()
    core_send("a", -1)
    by[1].end()
    core_send("b", 1)
    forward(-1)
    ax[1].end()
    core_send("a", 1)
    by[2].mid()
    ax[2].mid()
    forward(1)
    by[2].end()
    core_send("b", 2)
    ax[2].end()
    core_send("a", 2)
    for cp in misc:
        cp.wait()
    forward(2)

    RB = 64

    def head(i, carry):
        h, rb = i // 7, lax.rem(i, 7)
        rows = pl.ds(pl.multiple_of(rb * RB, RB), RB)
        cols = pl.ds(pl.multiple_of(h * 128, 128), 128)
        yv = acc[rows, cols]
        tv = acc[rows, pl.ds(pl.multiple_of(512 + h * 128, 128), 128)]
        w = upv[rows, cols].astype(F32) * gain[...]
        inv = lax.rsqrt(jnp.sum(yv * yv, axis=-1, keepdims=True) * (1.0 / 128) + 1e-06)
        cubed = inv * inv * inv
        along = jnp.sum(w * yv, axis=-1, keepdims=True)
        yt = jnp.sum(yv * tv, axis=-1, keepdims=True)
        along_dot = jnp.sum(w * tv, axis=-1, keepdims=True)
        k1 = cubed * along * (1.0 / 128)
        inv_dot = -cubed * yt * (1.0 / 128)
        k2 = (3.0 * inv * inv * inv_dot * along + cubed * along_dot) * (1.0 / 128)
        g = inv * w - yv * k1
        hv = inv_dot * w - (yv * k2 + tv * k1)
        low = lax.broadcasted_iota(jnp.int32, (RB, 128), 1) < 64
        gr = pltpu.roll(g, 64, axis=1)
        hr = pltpu.roll(hv, 64, axis=1)
        gs[h, rows, pl.ds(0, 128)] = jnp.where(low, g, hr).astype(BF16)
        gs[h, rows, pl.ds(128, 128)] = jnp.where(low, gr, hv).astype(BF16)
        return carry

    lax.fori_loop(0, 28, head, 0)

    u = (x, y)
    v_own = (y, x)

    def udev(k, d):
        return dev(dx=d) if k == 0 else dev(dy=d)

    def vdev(k, d):
        return dev(dy=d) if k == 0 else dev(dx=d)

    def tile(k, uq, v, cc):
        xi, yj = (uq, v) if k == 0 else (v, uq)
        return jnp.dot(at[k, xi, cc], gs[yj], preferred_element_type=F32)

    ds_order = (2, 1, -1, 0)
    core_rs = {}

    def part_p(k, i):
        if i >= 2:
            core_rs[k, i - 2].wait_send()
            sent[:] = [cp for cp in sent if cp is not core_rs[k, i - 2]]
        uq = m4(u[k] + ds_order[i])

        def body(v, carry):
            csend[k, i % 2, v] = tile(k, uq, v, 1 - c).astype(BF16)
            return carry

        lax.fori_loop(0, 4, body, 0)
        core_rs[k, i] = xfer(csend.at[k, i % 2], crecv.at[k, i], partner)

    half_base = {}

    def half_copy(k, v):
        device = udev(k, 1 - 2 * (v // 2))
        return rdma(rsend.at[k, 0, v], rech.at[k, v], device, half_base[k] + v)

    def part_far(k):
        core_rs[k, 0].wait_recv()
        half_base[k] = take(4)
        uq = m4(u[k] + 2)

        def body(v, carry):
            rsend[k, 0, v] = (tile(k, uq, v, c) + crecv[k, 0, v].astype(F32)).astype(BF16)
            half_copy(k, v).start()
            return carry

        lax.fori_loop(0, 4, body, 0)

    early, late = {}, {}
    zorder = (2, 1, -1, 0)

    def near_free(k, i):
        core_rs[k, i].wait_recv()
        d = ds_order[i]
        uq = m4(u[k] + d)
        v0 = 2 if d == 1 else 0

        def body(v, carry):
            rsend[k, i, v] = (tile(k, uq, v, c) + crecv[k, i, v].astype(F32)).astype(BF16)
            return carry

        lax.fori_loop(v0, v0 + 2, body, 0)
        early[k, i] = xfer(rsend.at[k, i, pl.ds(v0, 2)], recf.at[k, i - 1, pl.ds(v0, 2)], udev(k, d))

    def near_sum(k, i):
        d = ds_order[i]
        uq = m4(u[k] + d)
        v0 = 0 if d == 1 else 2
        half_copy(k, v0).wait_recv()
        half_copy(k, v0 + 1).wait_recv()

        def body(v, carry):
            rsend[k, i, v] = (tile(k, uq, v, c) + crecv[k, i, v].astype(F32) + rech[k, v].astype(F32)).astype(BF16)
            return carry

        lax.fori_loop(v0, v0 + 2, body, 0)
        for dz in zorder:
            rows = pl.ds(pl.multiple_of(m4(zh + dz) * 112, 16), 112)
            late[k, i, dz] = xfer(rsend.at[k, i, pl.ds(v0, 2), rows], recf.at[k, i - 1, pl.ds(v0, 2), rows], udev(k, d))

    def part_own(k):
        core_rs[k, 3].wait_recv()

        def body(v, carry):
            s_buf[k, v] = (tile(k, u[k], v, c) + crecv[k, 3, v].astype(F32)).astype(BF16)
            return carry

        lax.fori_loop(0, 4, body, 0)

    phase2 = {}

    def chunk_sum(k, dz):
        rows = pl.ds(pl.multiple_of(m4(zh + dz) * 112, 16), 112)
        for i in (1, 2):
            if dz == zorder[0]:
                early[k, i].wait_recv()
            late[k, i, dz].wait_recv()

        def body(v, carry):
            s_buf[k, v, rows] = (s_buf[k, v, rows].astype(F32) + recf[k, 0, v, rows].astype(F32)
                                 + recf[k, 1, v, rows].astype(F32)).astype(BF16)
            return carry

        lax.fori_loop(0, 4, body, 0)
        for d in (2, 1, 3):
            vq = m4(v_own[k] + d)
            phase2[k, dz, d] = xfer(s_buf.at[k, vq, rows], yrecv.at[k, d - 1, rows], vdev(k, d))

    zbase = (take(8), take(8))

    def z_copy(k, rows, target, cols):
        delta = lax.rem(z - target + 8, 8)
        return rdma(t_buf.at[k, rows, pl.ds(pl.multiple_of(cols * 128, 128), 128)],
                    zrecv.at[k, delta], dev_z(target), zbase[k] + delta)

    def chunk_z(k, dz):
        q = m4(zh + dz)
        rows = pl.ds(pl.multiple_of(q * 112, 16), 112)
        for d in (1, 2, 3):
            phase2[k, dz, d].wait_recv()
        total = s_buf[k, v_own[k], rows].astype(F32)
        for d in range(3):
            total = total + yrecv[k, d, rows].astype(F32)
        t_buf[k, rows] = total.astype(BF16)
        if dz == 0:
            z_copy(k, rows, 2 * zh + (1 - zl), 1 - zl).start()
        else:
            for l in range(2):
                z_copy(k, rows, 2 * q + l, jnp.int32(l)).start()

    part_p(0, 0)
    part_p(1, 0)
    part_far(0)
    part_far(1)
    part_p(0, 1)
    part_p(0, 2)
    part_p(1, 1)
    part_p(1, 2)
    near_free(0, 1)
    near_free(0, 2)
    near_free(1, 1)
    near_free(1, 2)
    part_p(0, 3)
    part_p(1, 3)
    near_sum(0, 1)
    near_sum(0, 2)
    near_sum(1, 1)
    near_sum(1, 2)
    part_own(0)
    part_own(1)
    for j, dz in enumerate(zorder):
        for k in range(2):
            chunk_sum(k, dz)
            if j:
                chunk_z(k, zorder[j - 1])
    for k in range(2):
        chunk_z(k, zorder[-1])

    own_rows = pl.ds(pl.multiple_of(zh * 112, 16), 112)
    for k in range(2):
        for d in range(1, 8):
            pltpu.make_async_remote_copy(
                src_ref=zrecv.at[k, 0], dst_ref=zrecv.at[k, d], send_sem=send_sems.at[zbase[k] + d],
                recv_sem=recv_sems.at[zbase[k] + d], device_id=partner, device_id_type=MESH).wait_recv()
        total = t_buf[k, own_rows, pl.ds(pl.multiple_of(zl * 128, 128), 128)].astype(F32)
        for d in range(1, 8):
            total = total + zrecv[k, d].astype(F32)
        rk = pl.ds(k * 112, 112)
        g = total[:, :64]
        hv = pltpu.roll(total, 64, axis=1)[:, :64]
        pc = wp[zh, x, c, rk, pl.ds(pl.multiple_of(512 + y * 128, 128), 128)].astype(F32)
        pcr = pltpu.roll(pc, 64, axis=1)
        pv = jnp.where(zl == 0, pc, pcr)[:, :64]
        nm = 0.965 * mom_v[rk, :] + 0.035 * g
        nc = 0.99 * cur_v[rk, :] + 0.01 * (pv * hv)
        out_m[rk, :] = nm
        out_c[rk, :] = nc
        out_u[rk, :] = jnp.clip(nm / jnp.maximum(0.5 * nc, 0.25), -1.0, 1.0)

    for cp in sent:
        cp.wait_send()
    for k in range(2):
        for v in range(4):
            half_copy(k, v).wait_send()
        for d in range(1, 8):
            pltpu.make_async_remote_copy(
                src_ref=zrecv.at[k, 0], dst_ref=zrecv.at[k, d], send_sem=send_sems.at[zbase[k] + d],
                recv_sem=recv_sems.at[zbase[k] + d], device_id=partner, device_id_type=MESH).wait_send()
    assert count[0] <= NX, count[0]


def on_device(acts, upstream, k_weight, probe, norm_gain, momentum, curvature):
    any_spec = pl.BlockSpec(memory_space=pl.ANY)
    vmem = pl.BlockSpec(memory_space=pltpu.VMEM)
    out = jax.ShapeDtypeStruct((224, 64), F32)
    return pl.pallas_call(
        kernel,
        out_shape=(out, out, out),
        in_specs=[any_spec] * 4 + [vmem] + [any_spec] * 2,
        out_specs=(vmem, vmem, vmem),
        scratch_shapes=[
            pltpu.VMEM((4, 4, 2, 224, 1024), BF16),
            pltpu.VMEM((TOK, D), BF16),
            pltpu.VMEM((2, 4, 2, 448, 448), BF16),
            pltpu.VMEM((TOK, 1024), F32),
            pltpu.VMEM((TOK, 512), BF16),
            pltpu.VMEM((4, TOK, 256), BF16),
            pltpu.VMEM((2, 2, 4, 448, 256), BF16),
            pltpu.VMEM((2, 4, 4, 448, 256), BF16),
            pltpu.VMEM((2, 3, 4, 448, 256), BF16),
            pltpu.VMEM((2, 4, 448, 256), BF16),
            pltpu.VMEM((2, 2, 4, 448, 256), BF16),
            pltpu.VMEM((2, 4, 448, 256), BF16),
            pltpu.VMEM((2, 3, 448, 256), BF16),
            pltpu.VMEM((2, 448, 256), BF16),
            pltpu.VMEM((2, 8, 112, 128), BF16),
            pltpu.VMEM((224, 64), F32),
            pltpu.VMEM((224, 64), F32),
            pltpu.SemaphoreType.DMA((NX,)),
            pltpu.SemaphoreType.DMA((NX,)),
            pltpu.SemaphoreType.DMA((16,)),
        ],
        compiler_params=pltpu.CompilerParams(
            collective_id=0, has_side_effects=True, vmem_limit_bytes=67043328),
    )(acts, upstream, k_weight, probe, norm_gain.reshape(1, 128), momentum, curvature)


def solution(mesh):
    return jax.shard_map(
        on_device,
        mesh=mesh,
        in_specs=(
            P(("dp", "fsdp"), None),
            P(("dp", "fsdp"), None),
            P("fsdp", None),
            P("fsdp", None),
            P(),
            P("fsdp", "dp"),
            P("fsdp", "dp"),
        ),
        out_specs=(P("fsdp", "dp"), P("fsdp", "dp"), P("fsdp", "dp")),
        check_vma=False,
    )
```

```python
import jax
import jax.numpy as jnp
from jax import lax
from jax.experimental import pallas as pl
from jax.experimental.pallas import tpu as pltpu
from jax.sharding import PartitionSpec as P

MESH = pl.DeviceIdType.MESH
F32 = jnp.float32
BF16 = jnp.bfloat16
TOK = 448
ROWS_A, ROWS_B, ROWS_C = 80, 96, 48
D = 7168
NX = 400


def kernel(acts, upstream, k_weight, probe, gain, out,
           wp, av, at, acc, upv, gs, csend, crecv, rsend, rech, recf, s_buf,
           yrecv, t_buf, zrecv, send_sems, recv_sems, loc_sems):
    dp = lax.axis_index("dp")
    fs = lax.axis_index("fsdp")
    y, zl = dp // 2, lax.rem(dp, 2)
    zh, x, c = fs // 8, lax.rem(fs // 2, 4), lax.rem(fs, 2)

    def m4(v):
        return lax.rem(v + 8, 4)

    def dev(dx=0, dy=0, dz=0):
        return (m4(y + dy) * 2 + zl, m4(zh + dz) * 8 + m4(x + dx) * 2 + c)

    def dev_z(z):
        return (y * 2 + lax.rem(z, 2), (z // 2) * 8 + x * 2 + c)

    partner = (dp, zh * 8 + x * 2 + (1 - c))
    z = 2 * zh + zl

    barrier = pltpu.get_barrier_semaphore()
    peers = [partner]
    for d in (1, 2, 3):
        peers += [dev(dx=d), dev(dy=d)]
    for d in range(1, 8):
        peers.append(dev_z(lax.rem(z + d, 8)))

    def local(src, dst, i):
        cp = pltpu.make_async_copy(src, dst, loc_sems.at[i])
        cp.start()
        return cp

    lo, hi, ends = pl.ds(0, ROWS_A), pl.ds(ROWS_A, ROWS_B), pl.ds(ROWS_A + ROWS_B, ROWS_C)
    quarter = wp.at[zh, x, c, hi, pl.ds(pl.multiple_of(y * 256, 256), 256)]
    part_cols = pl.ds(pl.multiple_of(lax.rem(y, 2) * 256, 256), 256)
    side = wp.at[zh, x, c, ends, pl.ds(pl.multiple_of(zl * 512, 512), 512)]

    @pl.when(y < 2)
    def _():
        pltpu.make_async_copy(k_weight.at[hi, part_cols], quarter, loc_sems.at[13]).start()

    @pl.when(y >= 2)
    def _():
        pltpu.make_async_copy(probe.at[hi, part_cols], quarter, loc_sems.at[13]).start()

    @pl.when(zl == 0)
    def _():
        pltpu.make_async_copy(k_weight.at[ends], side, loc_sems.at[14]).start()

    @pl.when(zl == 1)
    def _():
        pltpu.make_async_copy(probe.at[ends], side, loc_sems.at[14]).start()

    own = [local(k_weight.at[lo], wp.at[zh, x, c, lo, pl.ds(0, 512)], 0),
           local(probe.at[lo], wp.at[zh, x, c, lo, pl.ds(512, 512)], 1),
           pltpu.make_async_copy(k_weight.at[hi, part_cols], quarter, loc_sems.at[13]),
           pltpu.make_async_copy(k_weight.at[ends], side, loc_sems.at[14])]
    acp = [local(acts.at[:, pl.ds(i * 896, 896)], av.at[:, pl.ds(i * 896, 896)], 2 + i) for i in range(8)]
    misc = [local(upstream, upv, 10)]

    for p in peers:
        pl.semaphore_signal(barrier, inc=1, device_id=p, device_id_type=MESH)
    pl.semaphore_wait(barrier, len(peers))

    count = [0]
    sent = []

    def take(n):
        base = count[0]
        count[0] += n
        return base

    def rdma(src, dst, device, i):
        return pltpu.make_async_remote_copy(
            src_ref=src, dst_ref=dst, send_sem=send_sems.at[i], recv_sem=recv_sems.at[i],
            device_id=device, device_id_type=MESH)

    def xfer(src, dst, device):
        cp = rdma(src, dst, device, take(1))
        cp.start()
        sent.append(cp)
        return cp

    class Ring:
        def __init__(self, region, half, coord, up, down):
            self.region, self.half, self.coord, self.up, self.down = region, half, coord, up, down

        def start(self):
            r = self.region(self.coord)
            self.p = xfer(r, r, self.up)
            self.m = xfer(r, r, self.down)

        def mid(self):
            self.p.wait_recv()
            r = self.half(m4(self.coord - 1), 0)
            self.hp = xfer(r, r, self.up)
            self.m.wait_recv()
            r = self.half(m4(self.coord + 1), 1)
            self.hm = xfer(r, r, self.down)

        def end(self):
            self.hp.wait_recv()
            self.hm.wait_recv()

    class Ring8:
        def __init__(self, xq):
            self.xq = xq

        def block(self, zz, off=0, width=512):
            col = pl.multiple_of(lax.rem(zz, 2) * 512 + off, 128)
            return wp.at[zz // 2, self.xq, c, ends, pl.ds(col, width)]

        def hop(self, n):
            if n > 1:
                self.p.wait_recv()
                self.m.wait_recv()
            if n == 5:
                return
            low, high = lax.rem(z - n + 9, 8), lax.rem(z + n - 1, 8)
            width = 512 if n < 4 else 256
            r = self.block(low, 0, width)
            self.p = xfer(r, r, dev_z(lax.rem(z + 1, 8)))
            r = self.block(high, 512 - width, width)
            self.m = xfer(r, r, dev_z(lax.rem(z + 7, 8)))

    yc = pl.multiple_of(y * 256, 256)

    def bz_half(q, i):
        return wp.at[q, x, c, hi, pl.ds(pl.multiple_of(yc + i * 128, 128), 128)]

    bz = Ring(lambda q: wp.at[q, x, c, hi, pl.ds(yc, 256)], bz_half, zh, dev(dz=1), dev(dz=-1))
    az = Ring(lambda q: wp.at[q, x, c, lo, :],
              lambda q, i: wp.at[q, x, c, lo, pl.ds(i * 512, 512)], zh, dev(dz=1), dev(dz=-1))
    zc = pl.multiple_of(zl * 512, 512)
    cx = Ring(lambda q: wp.at[zh, q, c, ends, pl.ds(zc, 512)],
              lambda q, i: wp.at[zh, q, c, ends, pl.ds(pl.multiple_of(zc + i * 256, 256), 256)],
              x, dev(dx=1), dev(dx=-1))
    cz = {dx: Ring8(m4(x + dx)) for dx in (0, -1, 1, 2)}
    bx, ax, by = {}, {}, {}
    for dz in (0, -1, 1, 2):
        def mk(q):
            bx[dz] = Ring(lambda k: wp.at[q, k, c, hi, pl.ds(yc, 256)],
                          lambda k, i: wp.at[q, k, c, hi, pl.ds(pl.multiple_of(yc + i * 128, 128), 128)],
                          x, dev(dx=1), dev(dx=-1))
            ax[dz] = Ring(lambda k: wp.at[q, k, c, lo, :],
                          lambda k, i: wp.at[q, k, c, lo, pl.ds(i * 512, 512)],
                          x, dev(dx=1), dev(dx=-1))
            by[dz] = Ring(lambda k: wp.at[q, :, c, hi, pl.ds(pl.multiple_of(k * 256, 256), 256)],
                          lambda k, i: wp.at[q, pl.ds(2 * i, 2), c, hi, pl.ds(pl.multiple_of(k * 256, 256), 256)],
                          y, dev(dy=1), dev(dy=-1))
        mk(m4(zh + dz))

    core = {}

    def core_send(kind, dz):
        r = wp.at[m4(zh + dz), :, c, {"a": lo, "b": hi, "c": ends}[kind], :]
        core[kind, dz] = xfer(r, r, partner)

    def transpose(i):
        acp[i].wait()
        q, xp = i // 2, i % 2
        blk = av[:, i * 896:(i + 1) * 896]
        tr = blk.T
        for xx in range(2):
            for cc in range(2):
                for col in range(2):
                    r0 = xx * 448 + cc * 224 + col * 112
                    at[col, xp * 2 + xx, cc, pl.ds(q * 112, 112), :] = tr[r0:r0 + 112, :]

    first = [True]

    def forward(dz):
        core["a", dz].wait_recv()
        core["b", dz].wait_recv()
        core["c", dz].wait_recv()
        q = m4(zh + dz)
        init = first[0]
        first[0] = False
        for n in range(2):
            total = None if init else acc[:, n * 512:(n + 1) * 512]
            for xp in range(2):
                lhs = av[:, pl.ds(pl.multiple_of(q * 1792 + xp * 896, 128), 896)]
                rhs = wp[q, xp * 2:xp * 2 + 2, :, :, n * 512:(n + 1) * 512].reshape(896, 512)
                part = jnp.dot(lhs, rhs, preferred_element_type=F32)
                total = part if total is None else total + part
            acc[:, n * 512:(n + 1) * 512] = total

    for cp in own:
        cp.wait()
    bx[0].start()
    bz.start()
    az.start()
    transpose(0)
    ax[0].start()
    bx[0].mid()
    bz.mid()
    cx.start()
    bx[-1].start()
    bx[0].end()
    by[0].start()
    bx[1].start()
    cx.mid()
    cz[1].hop(1)
    bx[-1].mid()
    ax[0].mid()
    transpose(1)
    cz[0].hop(1)
    bx[1].mid()
    bx[-1].end()
    by[-1].start()
    az.mid()
    cx.end()
    ax[-1].start()
    cz[2].hop(1)
    transpose(2)
    cz[1].hop(2)
    bz.end()
    bx[2].start()
    ax[0].end()
    by[0].mid()
    transpose(3)
    ax[-1].mid()
    by[-1].mid()
    cz[-1].hop(1)
    transpose(4)
    bx[2].mid()
    cz[0].hop(2)
    ax[1].start()
    az.end()
    bx[1].end()
    cz[1].hop(3)
    core_send("a", 0)
    by[0].end()
    by[1].start()
    ax[2].start()
    cz[-1].hop(2)
    core_send("b", 0)
    ax[-1].end()
    transpose(5)
    cz[2].hop(2)
    cz[0].hop(3)
    by[-1].end()
    core_send("c", 0)
    transpose(6)
    bx[2].end()
    core_send("b", -1)
    cz[-1].hop(3)
    core_send("a", -1)
    by[2].start()
    ax[1].mid()
    cz[2].hop(3)
    cz[-1].hop(4)
    cz[1].hop(4)
    transpose(7)
    cz[2].hop(4)
    cz[0].hop(4)
    core_send("c", -1)
    by[1].mid()
    core_send("c", 1)
    ax[2].mid()
    forward(0)
    by[2].mid()
    ax[1].end()
    core_send("a", 1)
    cz[2].hop(5)
    cz[-1].hop(5)
    cz[0].hop(5)
    cz[1].hop(5)
    by[1].end()
    core_send("b", 1)
    ax[2].end()
    core_send("c", 2)
    core_send("a", 2)
    forward(-1)
    by[2].end()
    core_send("b", 2)
    forward(1)
    forward(2)
    for cp in misc:
        cp.wait()

    RB = 64

    def head(i, carry):
        h, rb = i // 7, lax.rem(i, 7)
        rows = pl.ds(pl.multiple_of(rb * RB, RB), RB)
        cols = pl.ds(pl.multiple_of(h * 128, 128), 128)
        yv = acc[rows, cols]
        tv = acc[rows, pl.ds(pl.multiple_of(512 + h * 128, 128), 128)]
        w = upv[rows, cols].astype(F32) * gain[...]
        inv = lax.rsqrt(jnp.sum(yv * yv, axis=-1, keepdims=True) * (1.0 / 128) + 1e-06)
        cubed = inv * inv * inv
        along = jnp.sum(w * yv, axis=-1, keepdims=True)
        yt = jnp.sum(yv * tv, axis=-1, keepdims=True)
        along_dot = jnp.sum(w * tv, axis=-1, keepdims=True)
        k1 = cubed * along * (1.0 / 128)
        inv_dot = -cubed * yt * (1.0 / 128)
        k2 = (3.0 * inv * inv * inv_dot * along + cubed * along_dot) * (1.0 / 128)
        g = inv * w - yv * k1
        hv = inv_dot * w - (yv * k2 + tv * k1)
        low = lax.broadcasted_iota(jnp.int32, (RB, 128), 1) < 64
        gr = pltpu.roll(g, 64, axis=1)
        hr = pltpu.roll(hv, 64, axis=1)
        gs[h, rows, pl.ds(0, 128)] = jnp.where(low, g, hr).astype(BF16)
        gs[h, rows, pl.ds(128, 128)] = jnp.where(low, gr, hv).astype(BF16)
        return carry

    lax.fori_loop(0, 28, head, 0)

    u = (x, y)
    v_own = (y, x)

    def udev(k, d):
        return dev(dx=d) if k == 0 else dev(dy=d)

    def vdev(k, d):
        return dev(dy=d) if k == 0 else dev(dx=d)

    def tile(k, uq, v, cc):
        xi, yj = (uq, v) if k == 0 else (v, uq)
        return jnp.dot(at[k, xi, cc], gs[yj], preferred_element_type=F32)

    ds_order = (2, 1, -1, 0)
    core_rs = {}

    def part_p(k, i):
        if i >= 2:
            core_rs[k, i - 2].wait_send()
            sent[:] = [cp for cp in sent if cp is not core_rs[k, i - 2]]
        uq = m4(u[k] + ds_order[i])

        def body(v, carry):
            csend[k, i % 2, v] = tile(k, uq, v, 1 - c).astype(BF16)
            return carry

        lax.fori_loop(0, 4, body, 0)
        core_rs[k, i] = xfer(csend.at[k, i % 2], crecv.at[k, i], partner)

    half_base = {}

    def half_copy(k, v):
        device = udev(k, 1 - 2 * (v // 2))
        return rdma(rsend.at[k, 0, v], rech.at[k, v], device, half_base[k] + v)

    def part_far(k):
        core_rs[k, 0].wait_recv()
        half_base[k] = take(4)
        uq = m4(u[k] + 2)

        def body(v, carry):
            rsend[k, 0, v] = (tile(k, uq, v, c) + crecv[k, 0, v].astype(F32)).astype(BF16)
            half_copy(k, v).start()
            return carry

        lax.fori_loop(0, 4, body, 0)

    early, late = {}, {}
    zorder = (2, 1, -1, 0)

    def near_free(k, i):
        core_rs[k, i].wait_recv()
        d = ds_order[i]
        uq = m4(u[k] + d)
        v0 = 2 if d == 1 else 0

        def body(v, carry):
            rsend[k, i, v] = (tile(k, uq, v, c) + crecv[k, i, v].astype(F32)).astype(BF16)
            return carry

        lax.fori_loop(v0, v0 + 2, body, 0)
        early[k, i] = xfer(rsend.at[k, i, pl.ds(v0, 2)], recf.at[k, i - 1, pl.ds(v0, 2)], udev(k, d))

    def near_sum(k, i):
        d = ds_order[i]
        uq = m4(u[k] + d)
        v0 = 0 if d == 1 else 2
        half_copy(k, v0).wait_recv()
        half_copy(k, v0 + 1).wait_recv()

        def body(v, carry):
            rsend[k, i, v] = (tile(k, uq, v, c) + crecv[k, i, v].astype(F32) + rech[k, v].astype(F32)).astype(BF16)
            return carry

        lax.fori_loop(v0, v0 + 2, body, 0)
        for dz in zorder:
            rows = pl.ds(pl.multiple_of(m4(zh + dz) * 112, 16), 112)
            late[k, i, dz] = xfer(rsend.at[k, i, pl.ds(v0, 2), rows], recf.at[k, i - 1, pl.ds(v0, 2), rows], udev(k, d))

    def part_own(k):
        core_rs[k, 3].wait_recv()

        def body(v, carry):
            s_buf[k, v] = (tile(k, u[k], v, c) + crecv[k, 3, v].astype(F32)).astype(BF16)
            return carry

        lax.fori_loop(0, 4, body, 0)

    phase2 = {}

    def chunk_sum(k, dz):
        rows = pl.ds(pl.multiple_of(m4(zh + dz) * 112, 16), 112)
        for i in (1, 2):
            if dz == zorder[0]:
                early[k, i].wait_recv()
            late[k, i, dz].wait_recv()

        def body(v, carry):
            s_buf[k, v, rows] = (s_buf[k, v, rows].astype(F32) + recf[k, 0, v, rows].astype(F32)
                                 + recf[k, 1, v, rows].astype(F32)).astype(BF16)
            return carry

        lax.fori_loop(0, 4, body, 0)
        for d in (2, 1, 3):
            vq = m4(v_own[k] + d)
            phase2[k, dz, d] = xfer(s_buf.at[k, vq, rows], yrecv.at[k, d - 1, rows], vdev(k, d))

    zbase = (take(8), take(8))

    def z_copy(k, rows, target, cols):
        delta = lax.rem(z - target + 8, 8)
        return rdma(t_buf.at[k, rows, pl.ds(pl.multiple_of(cols * 128, 128), 128)],
                    zrecv.at[k, delta], dev_z(target), zbase[k] + delta)

    def chunk_z(k, dz):
        q = m4(zh + dz)
        rows = pl.ds(pl.multiple_of(q * 112, 16), 112)
        for d in (1, 2, 3):
            phase2[k, dz, d].wait_recv()
        total = s_buf[k, v_own[k], rows].astype(F32)
        for d in range(3):
            total = total + yrecv[k, d, rows].astype(F32)
        t_buf[k, rows] = total.astype(BF16)
        if dz == 0:
            z_copy(k, rows, 2 * zh + (1 - zl), 1 - zl).start()
        else:
            for l in range(2):
                z_copy(k, rows, 2 * q + l, jnp.int32(l)).start()

    part_p(0, 0)
    part_p(1, 0)
    part_far(0)
    part_far(1)
    part_p(0, 1)
    part_p(0, 2)
    part_p(1, 1)
    part_p(1, 2)
    near_free(0, 1)
    near_free(0, 2)
    near_free(1, 1)
    near_free(1, 2)
    part_p(0, 3)
    part_p(1, 3)
    near_sum(0, 1)
    near_sum(0, 2)
    near_sum(1, 1)
    near_sum(1, 2)
    part_own(0)
    part_own(1)
    for j, dz in enumerate(zorder):
        for k in range(2):
            chunk_sum(k, dz)
            if j:
                chunk_z(k, zorder[j - 1])
    for k in range(2):
        chunk_z(k, zorder[-1])

    sums = []
    own_rows = pl.ds(pl.multiple_of(zh * 112, 16), 112)
    for k in range(2):
        for d in range(1, 8):
            pltpu.make_async_remote_copy(
                src_ref=zrecv.at[k, 0], dst_ref=zrecv.at[k, d], send_sem=send_sems.at[zbase[k] + d],
                recv_sem=recv_sems.at[zbase[k] + d], device_id=partner, device_id_type=MESH).wait_recv()
        total = t_buf[k, own_rows, pl.ds(pl.multiple_of(zl * 128, 128), 128)].astype(F32)
        for d in range(1, 8):
            total = total + zrecv[k, d].astype(F32)
        sums.append(total)
    total = jnp.concatenate(sums, axis=0).T
    head_cols = pl.ds(pl.multiple_of(512 + y * 128, 128), 128)
    probe_t = wp[zh, x, c, :, head_cols].astype(F32).T
    out[pl.ds(0, 64), :] = total[:64]
    out[pl.ds(64, 64), :] = total[64:] * jnp.where(zl == 0, probe_t[:64], probe_t[64:])

    for cp in sent:
        cp.wait_send()
    for k in range(2):
        for v in range(4):
            half_copy(k, v).wait_send()
        for d in range(1, 8):
            pltpu.make_async_remote_copy(
                src_ref=zrecv.at[k, 0], dst_ref=zrecv.at[k, d], send_sem=send_sems.at[zbase[k] + d],
                recv_sem=recv_sems.at[zbase[k] + d], device_id=partner, device_id_type=MESH).wait_send()
    assert count[0] <= NX, count[0]


def on_device(acts, upstream, k_weight, probe, norm_gain, momentum, curvature):
    any_spec = pl.BlockSpec(memory_space=pl.ANY)
    vmem = pl.BlockSpec(memory_space=pltpu.VMEM)
    sums = pl.pallas_call(
        kernel,
        out_shape=jax.ShapeDtypeStruct((128, 224), F32),
        in_specs=[any_spec] * 4 + [vmem],
        out_specs=vmem,
        scratch_shapes=[
            pltpu.VMEM((4, 4, 2, 224, 1024), BF16),
            pltpu.VMEM((TOK, D), BF16),
            pltpu.VMEM((2, 4, 2, 448, 448), BF16),
            pltpu.VMEM((TOK, 1024), F32),
            pltpu.VMEM((TOK, 512), BF16),
            pltpu.VMEM((4, TOK, 256), BF16),
            pltpu.VMEM((2, 2, 4, 448, 256), BF16),
            pltpu.VMEM((2, 4, 4, 448, 256), BF16),
            pltpu.VMEM((2, 3, 4, 448, 256), BF16),
            pltpu.VMEM((2, 4, 448, 256), BF16),
            pltpu.VMEM((2, 2, 4, 448, 256), BF16),
            pltpu.VMEM((2, 4, 448, 256), BF16),
            pltpu.VMEM((2, 3, 448, 256), BF16),
            pltpu.VMEM((2, 448, 256), BF16),
            pltpu.VMEM((2, 8, 112, 128), BF16),
            pltpu.SemaphoreType.DMA((NX,)),
            pltpu.SemaphoreType.DMA((NX,)),
            pltpu.SemaphoreType.DMA((16,)),
        ],
        compiler_params=pltpu.CompilerParams(
            collective_id=0, has_side_effects=True, vmem_limit_bytes=67043328),
    )(acts, upstream, k_weight, probe, norm_gain.reshape(1, 128))
    new_momentum = 0.965 * momentum.T + 0.035 * sums[:64]
    new_curvature = 0.99 * curvature.T + 0.01 * sums[64:]
    update = jnp.clip(new_momentum / jnp.maximum(0.5 * new_curvature, 0.25), -1.0, 1.0)
    return (new_momentum.T, new_curvature.T, update.T)


def solution(mesh):
    return jax.shard_map(
        on_device,
        mesh=mesh,
        in_specs=(
            P(("dp", "fsdp"), None),
            P(("dp", "fsdp"), None),
            P("fsdp", None),
            P("fsdp", None),
            P(),
            P("fsdp", "dp"),
            P("fsdp", "dp"),
        ),
        out_specs=(P("fsdp", "dp"), P("fsdp", "dp"), P("fsdp", "dp")),
        check_vma=False,
    )
```

```python
import jax
import jax.numpy as jnp
from jax import lax
from jax.experimental import pallas as pl
from jax.experimental.pallas import tpu as pltpu
from jax.sharding import PartitionSpec as P

MESH = pl.DeviceIdType.MESH
F32 = jnp.float32
BF16 = jnp.bfloat16
TOK = 448
RA = 80
RC = 224 - 2 * RA
ROWS_A, ROWS_B, ROWS_C = 80, 96, 48
D = 7168
NX = 400


def kernel(acts, upstream, k_weight, probe, gain, out,
           wp, av, at, acc, upv, gs, csend, crecv, rsend, rech, recf, s_buf,
           far2, near2, t_buf, zrecv,
           at_z, zsend, zcrecv, o_buf, zfar, znear, xrecv, u_buf, y3recv, send_sems, recv_sems, loc_sems):
    dp = lax.axis_index("dp")
    fs = lax.axis_index("fsdp")
    y, zl = dp // 2, lax.rem(dp, 2)
    zh, x, c = fs // 8, lax.rem(fs // 2, 4), lax.rem(fs, 2)

    def m4(v):
        return lax.rem(v + 8, 4)

    def dev(dx=0, dy=0, dz=0):
        return (m4(y + dy) * 2 + zl, m4(zh + dz) * 8 + m4(x + dx) * 2 + c)

    def dev_z(z):
        return (y * 2 + lax.rem(z, 2), (z // 2) * 8 + x * 2 + c)

    partner = (dp, zh * 8 + x * 2 + (1 - c))
    z = 2 * zh + zl

    barrier = pltpu.get_barrier_semaphore()
    peers = [partner]
    for d in (1, 2, 3):
        peers += [dev(dx=d), dev(dy=d)]
    for d in range(1, 8):
        peers.append(dev_z(lax.rem(z + d, 8)))

    def local(src, dst, i):
        cp = pltpu.make_async_copy(src, dst, loc_sems.at[i])
        cp.start()
        return cp

    lo, hi, ends = pl.ds(0, ROWS_A), pl.ds(ROWS_A, ROWS_B), pl.ds(ROWS_A + ROWS_B, ROWS_C)
    quarter = wp.at[zh, x, c, hi, pl.ds(pl.multiple_of(y * 256, 256), 256)]
    part_cols = pl.ds(pl.multiple_of(lax.rem(y, 2) * 256, 256), 256)
    side = wp.at[zh, x, c, ends, pl.ds(pl.multiple_of(zl * 512, 512), 512)]

    @pl.when(y < 2)
    def _():
        pltpu.make_async_copy(k_weight.at[hi, part_cols], quarter, loc_sems.at[13]).start()

    @pl.when(y >= 2)
    def _():
        pltpu.make_async_copy(probe.at[hi, part_cols], quarter, loc_sems.at[13]).start()

    @pl.when(zl == 0)
    def _():
        pltpu.make_async_copy(k_weight.at[ends], side, loc_sems.at[14]).start()

    @pl.when(zl == 1)
    def _():
        pltpu.make_async_copy(probe.at[ends], side, loc_sems.at[14]).start()

    own = [local(k_weight.at[lo], wp.at[zh, x, c, lo, pl.ds(0, 512)], 0),
           local(probe.at[lo], wp.at[zh, x, c, lo, pl.ds(512, 512)], 1),
           pltpu.make_async_copy(k_weight.at[hi, part_cols], quarter, loc_sems.at[13]),
           pltpu.make_async_copy(k_weight.at[ends], side, loc_sems.at[14])]
    acp = [local(acts.at[:, pl.ds(i * 896, 896)], av.at[:, pl.ds(i * 896, 896)], 2 + i) for i in range(8)]
    misc = [local(upstream, upv, 10)]

    for p in peers:
        pl.semaphore_signal(barrier, inc=1, device_id=p, device_id_type=MESH)
    pl.semaphore_wait(barrier, len(peers))

    count = [0]
    sent = []

    def take(n):
        base = count[0]
        count[0] += n
        return base

    def rdma(src, dst, device, i):
        return pltpu.make_async_remote_copy(
            src_ref=src, dst_ref=dst, send_sem=send_sems.at[i], recv_sem=recv_sems.at[i],
            device_id=device, device_id_type=MESH)

    def xfer(src, dst, device):
        cp = rdma(src, dst, device, take(1))
        cp.start()
        sent.append(cp)
        return cp

    class Ring:
        def __init__(self, region, half, coord, up, down):
            self.region, self.half, self.coord, self.up, self.down = region, half, coord, up, down

        def start(self):
            r = self.region(self.coord)
            self.p = xfer(r, r, self.up)
            self.m = xfer(r, r, self.down)

        def mid(self):
            self.p.wait_recv()
            r = self.half(m4(self.coord - 1), 0)
            self.hp = xfer(r, r, self.up)
            self.m.wait_recv()
            r = self.half(m4(self.coord + 1), 1)
            self.hm = xfer(r, r, self.down)

        def end(self):
            self.hp.wait_recv()
            self.hm.wait_recv()

    class Ring8:
        def __init__(self, xq):
            self.xq = xq

        def block(self, zz, off=0, width=512):
            col = pl.multiple_of(lax.rem(zz, 2) * 512 + off, 128)
            return wp.at[zz // 2, self.xq, c, ends, pl.ds(col, width)]

        def hop(self, n):
            if n > 1:
                self.p.wait_recv()
                self.m.wait_recv()
            if n == 5:
                return
            low, high = lax.rem(z - n + 9, 8), lax.rem(z + n - 1, 8)
            width = 512 if n < 4 else 256
            r = self.block(low, 0, width)
            self.p = xfer(r, r, dev_z(lax.rem(z + 1, 8)))
            r = self.block(high, 512 - width, width)
            self.m = xfer(r, r, dev_z(lax.rem(z + 7, 8)))

    yc = pl.multiple_of(y * 256, 256)

    def bz_half(q, i):
        return wp.at[q, x, c, hi, pl.ds(pl.multiple_of(yc + i * 128, 128), 128)]

    bz = Ring(lambda q: wp.at[q, x, c, hi, pl.ds(yc, 256)], bz_half, zh, dev(dz=1), dev(dz=-1))
    az = Ring(lambda q: wp.at[q, x, c, lo, :],
              lambda q, i: wp.at[q, x, c, lo, pl.ds(i * 512, 512)], zh, dev(dz=1), dev(dz=-1))
    zc = pl.multiple_of(zl * 512, 512)
    cx = Ring(lambda q: wp.at[zh, q, c, ends, pl.ds(zc, 512)],
              lambda q, i: wp.at[zh, q, c, ends, pl.ds(pl.multiple_of(zc + i * 256, 256), 256)],
              x, dev(dx=1), dev(dx=-1))
    cz = {dx: Ring8(m4(x + dx)) for dx in (0, -1, 1, 2)}
    bx, ax, by = {}, {}, {}
    for dz in (0, -1, 1, 2):
        def mk(q):
            bx[dz] = Ring(lambda k: wp.at[q, k, c, hi, pl.ds(yc, 256)],
                          lambda k, i: wp.at[q, k, c, hi, pl.ds(pl.multiple_of(yc + i * 128, 128), 128)],
                          x, dev(dx=1), dev(dx=-1))
            ax[dz] = Ring(lambda k: wp.at[q, k, c, lo, :],
                          lambda k, i: wp.at[q, k, c, lo, pl.ds(i * 512, 512)],
                          x, dev(dx=1), dev(dx=-1))
            by[dz] = Ring(lambda k: wp.at[q, :, c, hi, pl.ds(pl.multiple_of(k * 256, 256), 256)],
                          lambda k, i: wp.at[q, pl.ds(2 * i, 2), c, hi, pl.ds(pl.multiple_of(k * 256, 256), 256)],
                          y, dev(dy=1), dev(dy=-1))
        mk(m4(zh + dz))

    core = {}

    def core_send(kind, dz):
        r = wp.at[m4(zh + dz), :, c, {"a": lo, "b": hi, "c": ends}[kind], :]
        core[kind, dz] = xfer(r, r, partner)

    def transpose(i):
        acp[i].wait()
        q, xp = i // 2, i % 2
        blk = av[:, i * 896:(i + 1) * 896]
        tr = blk.T
        for xx in range(2):
            for cc in range(2):
                r0 = xx * 448 + cc * 224
                for col in range(2):
                    at[col, xp * 2 + xx, cc, pl.ds(q * RA, RA), :] = tr[r0 + col * RA:r0 + (col + 1) * RA, :]
                at_z[q, cc, pl.ds((xp * 2 + xx) * RC, RC), :] = tr[r0 + 2 * RA:r0 + 224, :]

    first = [True]

    def forward(dz):
        core["a", dz].wait_recv()
        core["b", dz].wait_recv()
        core["c", dz].wait_recv()
        q = m4(zh + dz)
        init = first[0]
        first[0] = False
        for n in range(2):
            total = None if init else acc[:, n * 512:(n + 1) * 512]
            for xp in range(2):
                lhs = av[:, pl.ds(pl.multiple_of(q * 1792 + xp * 896, 128), 896)]
                rhs = wp[q, xp * 2:xp * 2 + 2, :, :, n * 512:(n + 1) * 512].reshape(896, 512)
                part = jnp.dot(lhs, rhs, preferred_element_type=F32)
                total = part if total is None else total + part
            acc[:, n * 512:(n + 1) * 512] = total

    for cp in own:
        cp.wait()
    bx[0].start()
    bz.start()
    az.start()
    transpose(0)
    ax[0].start()
    bx[0].mid()
    bz.mid()
    cx.start()
    bx[-1].start()
    bx[0].end()
    by[0].start()
    bx[1].start()
    cx.mid()
    cz[1].hop(1)
    bx[-1].mid()
    ax[0].mid()
    transpose(1)
    cz[0].hop(1)
    bx[1].mid()
    bx[-1].end()
    by[-1].start()
    az.mid()
    cx.end()
    ax[-1].start()
    cz[2].hop(1)
    transpose(2)
    cz[1].hop(2)
    bz.end()
    bx[2].start()
    ax[0].end()
    by[0].mid()
    transpose(3)
    ax[-1].mid()
    by[-1].mid()
    cz[-1].hop(1)
    transpose(4)
    bx[2].mid()
    cz[0].hop(2)
    ax[1].start()
    az.end()
    bx[1].end()
    cz[1].hop(3)
    core_send("a", 0)
    by[0].end()
    by[1].start()
    ax[2].start()
    cz[-1].hop(2)
    core_send("b", 0)
    ax[-1].end()
    transpose(5)
    cz[2].hop(2)
    cz[0].hop(3)
    by[-1].end()
    core_send("c", 0)
    transpose(6)
    bx[2].end()
    core_send("b", -1)
    cz[-1].hop(3)
    core_send("a", -1)
    by[2].start()
    ax[1].mid()
    cz[2].hop(3)
    cz[-1].hop(4)
    cz[1].hop(4)
    transpose(7)
    cz[2].hop(4)
    cz[0].hop(4)
    core_send("c", -1)
    by[1].mid()
    core_send("c", 1)
    ax[2].mid()
    forward(0)
    by[2].mid()
    ax[1].end()
    core_send("a", 1)
    cz[2].hop(5)
    cz[-1].hop(5)
    cz[0].hop(5)
    cz[1].hop(5)
    by[1].end()
    core_send("b", 1)
    ax[2].end()
    core_send("c", 2)
    core_send("a", 2)
    forward(-1)
    by[2].end()
    core_send("b", 2)
    forward(1)
    forward(2)
    for cp in misc:
        cp.wait()

    RB = 64

    def head(i, carry):
        h, rb = i // 7, lax.rem(i, 7)
        rows = pl.ds(pl.multiple_of(rb * RB, RB), RB)
        cols = pl.ds(pl.multiple_of(h * 128, 128), 128)
        yv = acc[rows, cols]
        tv = acc[rows, pl.ds(pl.multiple_of(512 + h * 128, 128), 128)]
        w = upv[rows, cols].astype(F32) * gain[...]
        inv = lax.rsqrt(jnp.sum(yv * yv, axis=-1, keepdims=True) * (1.0 / 128) + 1e-06)
        cubed = inv * inv * inv
        along = jnp.sum(w * yv, axis=-1, keepdims=True)
        yt = jnp.sum(yv * tv, axis=-1, keepdims=True)
        along_dot = jnp.sum(w * tv, axis=-1, keepdims=True)
        k1 = cubed * along * (1.0 / 128)
        inv_dot = -cubed * yt * (1.0 / 128)
        k2 = (3.0 * inv * inv * inv_dot * along + cubed * along_dot) * (1.0 / 128)
        g = inv * w - yv * k1
        hv = inv_dot * w - (yv * k2 + tv * k1)
        low = lax.broadcasted_iota(jnp.int32, (RB, 128), 1) < 64
        gr = pltpu.roll(g, 64, axis=1)
        hr = pltpu.roll(hv, 64, axis=1)
        gs[h, rows, pl.ds(0, 128)] = jnp.where(low, g, hr).astype(BF16)
        gs[h, rows, pl.ds(128, 128)] = jnp.where(low, gr, hv).astype(BF16)
        return carry

    lax.fori_loop(0, 28, head, 0)

    u = (x, y)
    v_own = (y, x)

    def udev(k, d):
        return dev(dx=d) if k == 0 else dev(dy=d)

    def vdev(k, d):
        return dev(dy=d) if k == 0 else dev(dx=d)

    def tile(k, uq, v, cc):
        xi, yj = (uq, v) if k == 0 else (v, uq)
        return jnp.dot(at[k, xi, cc], gs[yj], preferred_element_type=F32)

    def rows_of(dz):
        return pl.ds(pl.multiple_of(m4(zh + dz) * RA, 16), RA)

    step_of = {2: 0, 1: 1, -1: 2, 0: 3}
    core_rs = {}

    def part_p(k, d):
        i = step_of[d]
        if i >= 2:
            old = core_rs[k, i - 2]
            old.wait_send()
            sent[:] = [cp for cp in sent if cp is not old]
        uq = m4(u[k] + d)

        def body(v, carry):
            csend[k, i % 2, v] = tile(k, uq, v, 1 - c).astype(BF16)
            return carry

        lax.fori_loop(0, 4, body, 0)
        core_rs[k, i] = xfer(csend.at[k, i % 2], crecv.at[k, i], partner)

    halves = {}

    def far(k):
        core_rs[k, 0].wait_recv()
        uq = m4(u[k] + 2)

        def body(v, carry):
            rsend[k, 0, v] = (tile(k, uq, v, c) + crecv[k, 0, v].astype(F32)).astype(BF16)
            return carry

        for p in range(2):
            lax.fori_loop(2 * p, 2 * p + 2, body, 0)
            halves[k, p] = xfer(rsend.at[k, 0, pl.ds(2 * p, 2)], rech.at[k, pl.ds(2 * p, 2)], udev(k, 1 - 2 * p))

    early, late = {}, {}

    def near_free(k, d):
        i = step_of[d]
        core_rs[k, i].wait_recv()
        uq = m4(u[k] + d)
        v0 = 2 if d == 1 else 0

        def body(v, carry):
            rsend[k, i, v] = (tile(k, uq, v, c) + crecv[k, i, v].astype(F32)).astype(BF16)
            return carry

        lax.fori_loop(v0, v0 + 2, body, 0)
        early[k, i] = xfer(rsend.at[k, i, pl.ds(v0, 2)], recf.at[k, i - 1, pl.ds(v0, 2)], udev(k, d))

    def near_sum(k, d):
        i = step_of[d]
        uq = m4(u[k] + d)
        v0 = 0 if d == 1 else 2
        halves[k, v0 // 2].wait_recv()

        def body(v, carry):
            rsend[k, i, v] = (tile(k, uq, v, c) + crecv[k, i, v].astype(F32) + rech[k, v].astype(F32)).astype(BF16)
            return carry

        lax.fori_loop(v0, v0 + 2, body, 0)
        for dz in (2, 1, -1, 0):
            rows = rows_of(dz)
            late[k, i, dz] = xfer(rsend.at[k, i, pl.ds(v0, 2), rows], recf.at[k, i - 1, pl.ds(v0, 2), rows], udev(k, d))

    def part_own(k):
        core_rs[k, 3].wait_recv()

        def body(v, carry):
            s_buf[k, v] = (tile(k, u[k], v, c) + crecv[k, 3, v].astype(F32)).astype(BF16)
            return carry

        lax.fori_loop(0, 4, body, 0)

    second = {}
    seen = set()

    def chunk_sum(k, dz):
        rows = rows_of(dz)
        for i in (1, 2):
            if (k, i) not in seen:
                early[k, i].wait_recv()
                seen.add((k, i))
            late[k, i, dz].wait_recv()

        def body(v, carry):
            s_buf[k, v, rows] = (s_buf[k, v, rows].astype(F32) + recf[k, 0, v, rows].astype(F32)
                                 + recf[k, 1, v, rows].astype(F32)).astype(BF16)
            return carry

        lax.fori_loop(0, 4, body, 0)
        vq = m4(v_own[k] + 2)
        for p in range(2):
            second[k, dz, p] = xfer(s_buf.at[k, vq, rows, pl.ds(128 * p, 128)], far2.at[k, p, rows], vdev(k, 1 - 2 * p))

    def chunk_mid(k, dz):
        rows = rows_of(dz)
        for p in range(2):
            second[k, dz, p].wait_recv()
            vq = m4(v_own[k] + 1 - 2 * p)
            cols = pl.ds(128 * p, 128)
            s_buf[k, vq, rows, cols] = (s_buf[k, vq, rows, cols].astype(F32) + far2[k, p, rows].astype(F32)).astype(BF16)
            second[k, dz, 2 + p] = xfer(s_buf.at[k, vq, rows], near2.at[k, p, rows], vdev(k, 1 - 2 * p))

    zbase = (take(8), take(8))

    def z_copy(k, rows, target, cols):
        delta = lax.rem(z - target + 8, 8)
        return rdma(t_buf.at[k, rows, pl.ds(pl.multiple_of(cols * 128, 128), 128)],
                    zrecv.at[k, delta], dev_z(target), zbase[k] + delta)

    def chunk_z(k, dz):
        q = m4(zh + dz)
        rows = rows_of(dz)
        second[k, dz, 2].wait_recv()
        second[k, dz, 3].wait_recv()
        t_buf[k, rows] = (s_buf[k, v_own[k], rows].astype(F32) + near2[k, 0, rows].astype(F32)
                          + near2[k, 1, rows].astype(F32)).astype(BF16)
        if dz == 0:
            z_copy(k, rows, 2 * zh + (1 - zl), 1 - zl).start()
        else:
            for l in range(2):
                z_copy(k, rows, 2 * q + l, jnp.int32(l)).start()

    core_z = {}

    def part_pz(dz):
        q = m4(zh + dz)

        def body(j, carry):
            zsend[q, j] = jnp.dot(at_z[q, 1 - c], gs[j], preferred_element_type=F32).astype(BF16)
            return carry

        lax.fori_loop(0, 4, body, 0)
        core_z[dz] = xfer(zsend.at[q], zcrecv.at[q], partner)

    def part_oz(dz):
        q = m4(zh + dz)
        core_z[dz].wait_recv()

        def body(j, carry):
            o_buf[q, j] = (jnp.dot(at_z[q, c], gs[j], preferred_element_type=F32) + zcrecv[q, j].astype(F32)).astype(BF16)
            return carry

        lax.fori_loop(0, 4, body, 0)

    chain = {}
    up, down = dev_z(lax.rem(z + 1, 8)), dev_z(lax.rem(z + 7, 8))

    def z_block(zz):
        return zz // 2, pl.ds(pl.multiple_of(lax.rem(zz, 2) * 128, 128), 128)

    def add_z(zz, j, value):
        q, cols = z_block(zz)
        o_buf[q, j, :, cols] = (o_buf[q, j, :, cols].astype(F32) + value.astype(F32)).astype(BF16)

    def z_far():
        q, cols = z_block(lax.rem(z + 4, 8))
        for p, device in ((0, up), (1, down)):
            chain[4, p, p] = xfer(o_buf.at[q, pl.ds(2 * p, 2), :, cols], zfar.at[p], device)

    def z_step(n, h):
        for p, device in ((0, up), (1, down)):
            zz = lax.rem(z + 8 + (n if p == 0 else -n), 8)
            q, cols = z_block(zz)
            if n == 3:
                if h == p:
                    chain[4, p, p].wait_recv()
                    for j in range(2):
                        add_z(zz, 2 * p + j, zfar[p, j])
            else:
                chain[n + 1, p, h].wait_recv()
                for j in range(2):
                    add_z(zz, 2 * h + j, znear[p, 2 - n, 2 * h + j])
            chain[n, p, h] = xfer(o_buf.at[q, pl.ds(2 * h, 2), :, cols],
                                  znear.at[p, 3 - n, pl.ds(2 * h, 2)], device)

    def z_own(h):
        q, cols = z_block(z)
        for p in range(2):
            chain[1, p, h].wait_recv()
        for j in range(2 * h, 2 * h + 2):
            o_buf[q, j, :, cols] = (o_buf[q, j, :, cols].astype(F32) + znear[0, 2, j].astype(F32)
                                    + znear[1, 2, j].astype(F32)).astype(BF16)
        for d in (2, 1, 3):
            xq = m4(x + d)
            chain["x", d, h] = xfer(o_buf.at[q, pl.ds(2 * h, 2), pl.ds(pl.multiple_of(xq * RC, 16), RC), cols],
                                    xrecv.at[d - 1, pl.ds(2 * h, 2)], dev(dx=d))

    def z_x():
        q, cols = z_block(z)
        for d in (1, 2, 3):
            for h in range(2):
                chain["x", d, h].wait_recv()
        own_x = pl.ds(pl.multiple_of(x * RC, 16), RC)
        for j in range(4):
            total = o_buf[q, j, own_x, cols].astype(F32)
            for d in range(3):
                total = total + xrecv[d, j].astype(F32)
            u_buf[j] = total.astype(BF16)
        for d in (2, 1, 3):
            chain["y", d] = xfer(u_buf.at[m4(y + d)], y3recv.at[d - 1], dev(dy=d))

    part_p(0, 2)
    part_p(1, 2)
    part_p(1, 1)
    part_pz(2)
    far(0)
    far(1)
    part_p(0, 1)
    part_p(1, -1)
    near_free(1, 1)
    part_oz(2)
    z_far()
    near_free(0, 1)
    part_p(0, -1)
    part_pz(-1)
    part_pz(1)
    part_p(1, 0)
    near_free(1, -1)
    near_free(0, -1)
    part_oz(-1)
    part_oz(1)
    z_step(3, 1)
    part_pz(0)
    z_step(3, 0)
    near_sum(1, 1)
    near_sum(0, -1)
    near_sum(0, 1)
    z_step(2, 1)
    near_sum(1, -1)
    part_p(0, 0)
    part_own(1)
    part_oz(0)
    z_step(2, 0)
    part_own(0)
    z_step(1, 1)
    chunk_sum(1, 1)
    chunk_sum(1, 2)
    chunk_sum(0, 1)
    chunk_sum(1, -1)
    z_step(1, 0)
    chunk_mid(1, 1)
    chunk_sum(0, 2)
    chunk_mid(1, 2)
    chunk_sum(0, 0)
    chunk_mid(0, 1)
    chunk_sum(0, -1)
    chunk_mid(1, -1)
    chunk_mid(0, 2)
    chunk_sum(1, 0)
    chunk_z(1, 1)
    z_own(1)
    chunk_z(0, 1)
    z_own(0)
    chunk_mid(0, -1)
    chunk_z(1, 2)
    chunk_mid(1, 0)
    chunk_mid(0, 0)
    chunk_z(0, 2)
    chunk_z(0, -1)
    chunk_z(0, 0)
    chunk_z(1, -1)
    z_x()
    chunk_z(1, 0)

    sums = []
    own_rows = pl.ds(pl.multiple_of(zh * RA, 16), RA)
    for d in (1, 2, 3):
        chain["y", d].wait_recv()
    last = u_buf[y].astype(F32)
    for d in range(3):
        last = last + y3recv[d].astype(F32)
    for k in range(2):
        for d in range(1, 8):
            pltpu.make_async_remote_copy(
                src_ref=zrecv.at[k, 0], dst_ref=zrecv.at[k, d], send_sem=send_sems.at[zbase[k] + d],
                recv_sem=recv_sems.at[zbase[k] + d], device_id=partner, device_id_type=MESH).wait_recv()
        total = t_buf[k, own_rows, pl.ds(pl.multiple_of(zl * 128, 128), 128)].astype(F32)
        for d in range(1, 8):
            total = total + zrecv[k, d].astype(F32)
        sums.append(total)
    total = jnp.concatenate(sums + [last], axis=0).T
    head_cols = pl.ds(pl.multiple_of(512 + y * 128, 128), 128)
    probe_t = wp[zh, x, c, :, head_cols].astype(F32).T
    out[pl.ds(0, 64), :] = total[:64]
    out[pl.ds(64, 64), :] = total[64:] * jnp.where(zl == 0, probe_t[:64], probe_t[64:])

    for cp in sent:
        cp.wait_send()
    for k in range(2):
        for d in range(1, 8):
            pltpu.make_async_remote_copy(
                src_ref=zrecv.at[k, 0], dst_ref=zrecv.at[k, d], send_sem=send_sems.at[zbase[k] + d],
                recv_sem=recv_sems.at[zbase[k] + d], device_id=partner, device_id_type=MESH).wait_send()
    assert count[0] <= NX, count[0]


def on_device(acts, upstream, k_weight, probe, norm_gain, momentum, curvature):
    any_spec = pl.BlockSpec(memory_space=pl.ANY)
    vmem = pl.BlockSpec(memory_space=pltpu.VMEM)
    sums = pl.pallas_call(
        kernel,
        out_shape=jax.ShapeDtypeStruct((128, 224), F32),
        in_specs=[any_spec] * 4 + [vmem],
        out_specs=vmem,
        scratch_shapes=[
            pltpu.VMEM((4, 4, 2, 224, 1024), BF16),
            pltpu.VMEM((TOK, D), BF16),
            pltpu.VMEM((2, 4, 2, 4 * RA, TOK), BF16),
            pltpu.VMEM((TOK, 1024), F32),
            pltpu.VMEM((TOK, 512), BF16),
            pltpu.VMEM((4, TOK, 256), BF16),
            pltpu.VMEM((2, 2, 4, 4 * RA, 256), BF16),
            pltpu.VMEM((2, 4, 4, 4 * RA, 256), BF16),
            pltpu.VMEM((2, 3, 4, 4 * RA, 256), BF16),
            pltpu.VMEM((2, 4, 4 * RA, 256), BF16),
            pltpu.VMEM((2, 2, 4, 4 * RA, 256), BF16),
            pltpu.VMEM((2, 4, 4 * RA, 256), BF16),
            pltpu.VMEM((2, 2, 4 * RA, 128), BF16),
            pltpu.VMEM((2, 2, 4 * RA, 256), BF16),
            pltpu.VMEM((2, 4 * RA, 256), BF16),
            pltpu.VMEM((2, 8, RA, 128), BF16),
            pltpu.VMEM((4, 2, 4 * RC, TOK), BF16),
            pltpu.VMEM((4, 4, 4 * RC, 256), BF16),
            pltpu.VMEM((4, 4, 4 * RC, 256), BF16),
            pltpu.VMEM((4, 4, 4 * RC, 256), BF16),
            pltpu.VMEM((2, 2, 4 * RC, 128), BF16),
            pltpu.VMEM((2, 3, 4, 4 * RC, 128), BF16),
            pltpu.VMEM((3, 4, RC, 128), BF16),
            pltpu.VMEM((4, RC, 128), BF16),
            pltpu.VMEM((3, RC, 128), BF16),
            pltpu.SemaphoreType.DMA((NX,)),
            pltpu.SemaphoreType.DMA((NX,)),
            pltpu.SemaphoreType.DMA((16,)),
        ],
        compiler_params=pltpu.CompilerParams(
            collective_id=0, has_side_effects=True, vmem_limit_bytes=67043328),
    )(acts, upstream, k_weight, probe, norm_gain.reshape(1, 128))
    new_momentum = 0.965 * momentum.T + 0.035 * sums[:64]
    new_curvature = 0.99 * curvature.T + 0.01 * sums[64:]
    update = jnp.clip(new_momentum / jnp.maximum(0.5 * new_curvature, 0.25), -1.0, 1.0)
    return (new_momentum.T, new_curvature.T, update.T)


def solution(mesh):
    return jax.shard_map(
        on_device,
        mesh=mesh,
        in_specs=(
            P(("dp", "fsdp"), None),
            P(("dp", "fsdp"), None),
            P("fsdp", None),
            P("fsdp", None),
            P(),
            P("fsdp", "dp"),
            P("fsdp", "dp"),
        ),
        out_specs=(P("fsdp", "dp"), P("fsdp", "dp"), P("fsdp", "dp")),
        check_vma=False,
    )
```

```python
import jax
import jax.numpy as jnp
from jax import lax
from jax.experimental import pallas as pl
from jax.experimental.pallas import tpu as pltpu
from jax.sharding import PartitionSpec as P

MESH = pl.DeviceIdType.MESH
F32 = jnp.float32
BF16 = jnp.bfloat16
TOK = 448
RA = 80
RC = 224 - 2 * RA
ROWS_A, ROWS_B, ROWS_C = 80, 96, 48
D = 7168
NX = 400


def kernel(acts, upstream, k_weight, probe, gain, out,
           wp, av, at, acc, upv, gs, csend, crecv, rsend, rech, recf, s_buf,
           far2, near2, t_buf, zrecv,
           at_z, zsend, zcrecv, o_buf, zfar, znear, xrecv, u_buf, y3recv, send_sems, recv_sems, loc_sems):
    dp = lax.axis_index("dp")
    fs = lax.axis_index("fsdp")
    y, zl = dp // 2, lax.rem(dp, 2)
    zh, x, c = fs // 8, lax.rem(fs // 2, 4), lax.rem(fs, 2)

    def m4(v):
        return lax.rem(v + 8, 4)

    def dev(dx=0, dy=0, dz=0):
        return (m4(y + dy) * 2 + zl, m4(zh + dz) * 8 + m4(x + dx) * 2 + c)

    def dev_z(z):
        return (y * 2 + lax.rem(z, 2), (z // 2) * 8 + x * 2 + c)

    partner = (dp, zh * 8 + x * 2 + (1 - c))
    z = 2 * zh + zl

    barrier = pltpu.get_barrier_semaphore()
    peers = [partner]
    for d in (1, 2, 3):
        peers += [dev(dx=d), dev(dy=d)]
    for d in range(1, 8):
        peers.append(dev_z(lax.rem(z + d, 8)))

    def local(src, dst, i):
        cp = pltpu.make_async_copy(src, dst, loc_sems.at[i])
        cp.start()
        return cp

    lo, hi, ends = pl.ds(0, ROWS_A), pl.ds(ROWS_A, ROWS_B), pl.ds(ROWS_A + ROWS_B, ROWS_C)
    quarter = wp.at[zh, x, c, hi, pl.ds(pl.multiple_of(y * 256, 256), 256)]
    part_cols = pl.ds(pl.multiple_of(lax.rem(y, 2) * 256, 256), 256)
    side = wp.at[zh, x, c, ends, pl.ds(pl.multiple_of(zl * 512, 512), 512)]

    @pl.when(y < 2)
    def _():
        pltpu.make_async_copy(k_weight.at[hi, part_cols], quarter, loc_sems.at[13]).start()

    @pl.when(y >= 2)
    def _():
        pltpu.make_async_copy(probe.at[hi, part_cols], quarter, loc_sems.at[13]).start()

    @pl.when(zl == 0)
    def _():
        pltpu.make_async_copy(k_weight.at[ends], side, loc_sems.at[14]).start()

    @pl.when(zl == 1)
    def _():
        pltpu.make_async_copy(probe.at[ends], side, loc_sems.at[14]).start()

    own = [local(k_weight.at[lo], wp.at[zh, x, c, lo, pl.ds(0, 512)], 0),
           local(probe.at[lo], wp.at[zh, x, c, lo, pl.ds(512, 512)], 1),
           pltpu.make_async_copy(k_weight.at[hi, part_cols], quarter, loc_sems.at[13]),
           pltpu.make_async_copy(k_weight.at[ends], side, loc_sems.at[14])]
    acp = [local(acts.at[:, pl.ds(i * 896, 896)], av.at[:, pl.ds(i * 896, 896)], 2 + i) for i in range(8)]
    misc = [local(upstream, upv, 10)]

    for p in peers:
        pl.semaphore_signal(barrier, inc=1, device_id=p, device_id_type=MESH)
    pl.semaphore_wait(barrier, len(peers))

    count = [0]
    sent = []

    def take(n):
        base = count[0]
        count[0] += n
        return base

    def rdma(src, dst, device, i):
        return pltpu.make_async_remote_copy(
            src_ref=src, dst_ref=dst, send_sem=send_sems.at[i], recv_sem=recv_sems.at[i],
            device_id=device, device_id_type=MESH)

    def xfer(src, dst, device):
        cp = rdma(src, dst, device, take(1))
        cp.start()
        sent.append(cp)
        return cp

    class Ring:
        def __init__(self, region, half, coord, up, down):
            self.region, self.half, self.coord, self.up, self.down = region, half, coord, up, down

        def start(self):
            r = self.region(self.coord)
            self.p = xfer(r, r, self.up)
            self.m = xfer(r, r, self.down)

        def mid(self):
            self.p.wait_recv()
            r = self.half(m4(self.coord - 1), 0)
            self.hp = xfer(r, r, self.up)
            self.m.wait_recv()
            r = self.half(m4(self.coord + 1), 1)
            self.hm = xfer(r, r, self.down)

        def end(self):
            self.hp.wait_recv()
            self.hm.wait_recv()

    class Ring8:
        def __init__(self, xq):
            self.xq = xq

        def block(self, zz, off=0, width=512):
            col = pl.multiple_of(lax.rem(zz, 2) * 512 + off, 128)
            return wp.at[zz // 2, self.xq, c, ends, pl.ds(col, width)]

        def hop(self, n):
            if n > 1:
                self.p.wait_recv()
                self.m.wait_recv()
            if n == 5:
                return
            low, high = lax.rem(z - n + 9, 8), lax.rem(z + n - 1, 8)
            width = 512 if n < 4 else 256
            r = self.block(low, 0, width)
            self.p = xfer(r, r, dev_z(lax.rem(z + 1, 8)))
            r = self.block(high, 512 - width, width)
            self.m = xfer(r, r, dev_z(lax.rem(z + 7, 8)))

    yc = pl.multiple_of(y * 256, 256)

    def bz_half(q, i):
        return wp.at[q, x, c, hi, pl.ds(pl.multiple_of(yc + i * 128, 128), 128)]

    bz = Ring(lambda q: wp.at[q, x, c, hi, pl.ds(yc, 256)], bz_half, zh, dev(dz=1), dev(dz=-1))
    az = Ring(lambda q: wp.at[q, x, c, lo, :],
              lambda q, i: wp.at[q, x, c, lo, pl.ds(i * 512, 512)], zh, dev(dz=1), dev(dz=-1))
    zc = pl.multiple_of(zl * 512, 512)
    cx = Ring(lambda q: wp.at[zh, q, c, ends, pl.ds(zc, 512)],
              lambda q, i: wp.at[zh, q, c, ends, pl.ds(pl.multiple_of(zc + i * 256, 256), 256)],
              x, dev(dx=1), dev(dx=-1))
    cz = {dx: Ring8(m4(x + dx)) for dx in (0, -1, 1, 2)}
    bx, ax, by = {}, {}, {}
    for dz in (0, -1, 1, 2):
        def mk(q):
            bx[dz] = Ring(lambda k: wp.at[q, k, c, hi, pl.ds(yc, 256)],
                          lambda k, i: wp.at[q, k, c, hi, pl.ds(pl.multiple_of(yc + i * 128, 128), 128)],
                          x, dev(dx=1), dev(dx=-1))
            ax[dz] = Ring(lambda k: wp.at[q, k, c, lo, :],
                          lambda k, i: wp.at[q, k, c, lo, pl.ds(i * 512, 512)],
                          x, dev(dx=1), dev(dx=-1))
            by[dz] = Ring(lambda k: wp.at[q, :, c, hi, pl.ds(pl.multiple_of(k * 256, 256), 256)],
                          lambda k, i: wp.at[q, pl.ds(2 * i, 2), c, hi, pl.ds(pl.multiple_of(k * 256, 256), 256)],
                          y, dev(dy=1), dev(dy=-1))
        mk(m4(zh + dz))

    core = {}

    def core_send(kind, dz):
        r = wp.at[m4(zh + dz), :, c, {"a": lo, "b": hi, "c": ends}[kind], :]
        core[kind, dz] = xfer(r, r, partner)

    def transpose(i):
        acp[i].wait()
        q, xp = i // 2, i % 2
        blk = av[:, i * 896:(i + 1) * 896]
        tr = blk.T
        for xx in range(2):
            for cc in range(2):
                r0 = xx * 448 + cc * 224
                for col in range(2):
                    at[col, xp * 2 + xx, cc, pl.ds(q * RA, RA), :] = tr[r0 + col * RA:r0 + (col + 1) * RA, :]
                at_z[q, cc, pl.ds((xp * 2 + xx) * RC, RC), :] = tr[r0 + 2 * RA:r0 + 224, :]

    first = [True]

    def forward(dz):
        core["a", dz].wait_recv()
        core["b", dz].wait_recv()
        core["c", dz].wait_recv()
        q = m4(zh + dz)
        init = first[0]
        first[0] = False
        for n in range(2):
            total = None if init else acc[:, n * 512:(n + 1) * 512]
            for xp in range(2):
                lhs = av[:, pl.ds(pl.multiple_of(q * 1792 + xp * 896, 128), 896)]
                rhs = wp[q, xp * 2:xp * 2 + 2, :, :, n * 512:(n + 1) * 512].reshape(896, 512)
                part = jnp.dot(lhs, rhs, preferred_element_type=F32)
                total = part if total is None else total + part
            acc[:, n * 512:(n + 1) * 512] = total

    for cp in own:
        cp.wait()
    bz.start()
    bx[0].start()
    ax[0].start()
    transpose(0)
    az.start()
    bx[0].mid()
    bz.mid()
    bx[-1].start()
    transpose(1)
    cx.start()
    bx[1].start()
    bx[0].end()
    cz[0].hop(1)
    by[0].start()
    bx[-1].mid()
    cx.mid()
    ax[0].mid()
    cz[-1].hop(1)
    cz[1].hop(1)
    bx[-1].end()
    by[-1].start()
    bx[1].mid()
    az.mid()
    ax[1].start()
    transpose(2)
    bz.end()
    cx.end()
    cz[2].hop(1)
    transpose(3)
    bx[1].end()
    ax[0].end()
    bx[2].start()
    by[1].start()
    transpose(4)
    cz[0].hop(2)
    by[0].mid()
    ax[-1].start()
    ax[1].mid()
    cz[1].hop(2)
    cz[-1].hop(2)
    cz[2].hop(2)
    by[-1].mid()
    cz[0].hop(3)
    by[1].mid()
    bx[2].mid()
    core_send("a", 0)
    az.end()
    ax[2].start()
    cz[1].hop(3)
    transpose(5)
    cz[-1].hop(3)
    ax[1].end()
    cz[2].hop(3)
    core_send("c", 0)
    by[0].end()
    transpose(6)
    bx[2].end()
    core_send("b", 0)
    ax[-1].mid()
    by[2].start()
    by[-1].end()
    core_send("a", 1)
    cz[0].hop(4)
    cz[1].hop(4)
    transpose(7)
    core_send("b", -1)
    cz[-1].hop(4)
    ax[2].mid()
    by[1].end()
    core_send("b", 1)
    cz[2].hop(4)
    core_send("c", 1)
    core_send("c", -1)
    forward(0)
    by[2].mid()
    ax[2].end()
    ax[-1].end()
    cz[-1].hop(5)
    core_send("a", -1)
    cz[1].hop(5)
    core_send("a", 2)
    forward(1)
    cz[0].hop(5)
    cz[2].hop(5)
    core_send("c", 2)
    by[2].end()
    core_send("b", 2)
    forward(-1)
    forward(2)
    for cp in misc:
        cp.wait()

    RB = 64

    def head(i, carry):
        h, rb = i // 7, lax.rem(i, 7)
        rows = pl.ds(pl.multiple_of(rb * RB, RB), RB)
        cols = pl.ds(pl.multiple_of(h * 128, 128), 128)
        yv = acc[rows, cols]
        tv = acc[rows, pl.ds(pl.multiple_of(512 + h * 128, 128), 128)]
        w = upv[rows, cols].astype(F32) * gain[...]
        inv = lax.rsqrt(jnp.sum(yv * yv, axis=-1, keepdims=True) * (1.0 / 128) + 1e-06)
        cubed = inv * inv * inv
        along = jnp.sum(w * yv, axis=-1, keepdims=True)
        yt = jnp.sum(yv * tv, axis=-1, keepdims=True)
        along_dot = jnp.sum(w * tv, axis=-1, keepdims=True)
        k1 = cubed * along * (1.0 / 128)
        inv_dot = -cubed * yt * (1.0 / 128)
        k2 = (3.0 * inv * inv * inv_dot * along + cubed * along_dot) * (1.0 / 128)
        g = inv * w - yv * k1
        hv = inv_dot * w - (yv * k2 + tv * k1)
        low = lax.broadcasted_iota(jnp.int32, (RB, 128), 1) < 64
        gr = pltpu.roll(g, 64, axis=1)
        hr = pltpu.roll(hv, 64, axis=1)
        gs[h, rows, pl.ds(0, 128)] = jnp.where(low, g, hr).astype(BF16)
        gs[h, rows, pl.ds(128, 128)] = jnp.where(low, gr, hv).astype(BF16)
        return carry

    lax.fori_loop(0, 28, head, 0)

    u = (x, y)
    v_own = (y, x)

    def udev(k, d):
        return dev(dx=d) if k == 0 else dev(dy=d)

    def vdev(k, d):
        return dev(dy=d) if k == 0 else dev(dx=d)

    def tile(k, uq, v, cc):
        xi, yj = (uq, v) if k == 0 else (v, uq)
        return jnp.dot(at[k, xi, cc], gs[yj], preferred_element_type=F32)

    def rows_of(dz):
        return pl.ds(pl.multiple_of(m4(zh + dz) * RA, 16), RA)

    step_of = {2: 0, 1: 1, -1: 2, 0: 3}
    core_rs = {}

    def part_p(k, d):
        i = step_of[d]
        if i >= 2:
            old = core_rs[k, i - 2]
            old.wait_send()
            sent[:] = [cp for cp in sent if cp is not old]
        uq = m4(u[k] + d)

        def body(v, carry):
            csend[k, i % 2, v] = tile(k, uq, v, 1 - c).astype(BF16)
            return carry

        lax.fori_loop(0, 4, body, 0)
        core_rs[k, i] = xfer(csend.at[k, i % 2], crecv.at[k, i], partner)

    halves = {}

    def far(k):
        core_rs[k, 0].wait_recv()
        uq = m4(u[k] + 2)

        def body(v, carry):
            rsend[k, 0, v] = (tile(k, uq, v, c) + crecv[k, 0, v].astype(F32)).astype(BF16)
            return carry

        for p in range(2):
            lax.fori_loop(2 * p, 2 * p + 2, body, 0)
            halves[k, p] = xfer(rsend.at[k, 0, pl.ds(2 * p, 2)], rech.at[k, pl.ds(2 * p, 2)], udev(k, 1 - 2 * p))

    early, late = {}, {}

    def near_free(k, d):
        i = step_of[d]
        core_rs[k, i].wait_recv()
        uq = m4(u[k] + d)
        v0 = 2 if d == 1 else 0

        def body(v, carry):
            rsend[k, i, v] = (tile(k, uq, v, c) + crecv[k, i, v].astype(F32)).astype(BF16)
            return carry

        lax.fori_loop(v0, v0 + 2, body, 0)
        early[k, i] = xfer(rsend.at[k, i, pl.ds(v0, 2)], recf.at[k, i - 1, pl.ds(v0, 2)], udev(k, d))

    def near_sum(k, d):
        i = step_of[d]
        uq = m4(u[k] + d)
        v0 = 0 if d == 1 else 2
        halves[k, v0 // 2].wait_recv()

        def body(v, carry):
            rsend[k, i, v] = (tile(k, uq, v, c) + crecv[k, i, v].astype(F32) + rech[k, v].astype(F32)).astype(BF16)
            return carry

        lax.fori_loop(v0, v0 + 2, body, 0)
        for dz in (2, 1, -1, 0):
            rows = rows_of(dz)
            late[k, i, dz] = xfer(rsend.at[k, i, pl.ds(v0, 2), rows], recf.at[k, i - 1, pl.ds(v0, 2), rows], udev(k, d))

    def part_own(k):
        core_rs[k, 3].wait_recv()

        def body(v, carry):
            s_buf[k, v] = (tile(k, u[k], v, c) + crecv[k, 3, v].astype(F32)).astype(BF16)
            return carry

        lax.fori_loop(0, 4, body, 0)

    second = {}
    seen = set()

    def chunk_sum(k, dz):
        rows = rows_of(dz)
        for i in (1, 2):
            if (k, i) not in seen:
                early[k, i].wait_recv()
                seen.add((k, i))
            late[k, i, dz].wait_recv()

        def body(v, carry):
            s_buf[k, v, rows] = (s_buf[k, v, rows].astype(F32) + recf[k, 0, v, rows].astype(F32)
                                 + recf[k, 1, v, rows].astype(F32)).astype(BF16)
            return carry

        lax.fori_loop(0, 4, body, 0)
        vq = m4(v_own[k] + 2)
        for p in range(2):
            second[k, dz, p] = xfer(s_buf.at[k, vq, rows, pl.ds(128 * p, 128)], far2.at[k, p, rows], vdev(k, 1 - 2 * p))

    def chunk_mid(k, dz):
        rows = rows_of(dz)
        for p in range(2):
            second[k, dz, p].wait_recv()
            vq = m4(v_own[k] + 1 - 2 * p)
            cols = pl.ds(128 * p, 128)
            s_buf[k, vq, rows, cols] = (s_buf[k, vq, rows, cols].astype(F32) + far2[k, p, rows].astype(F32)).astype(BF16)
            second[k, dz, 2 + p] = xfer(s_buf.at[k, vq, rows], near2.at[k, p, rows], vdev(k, 1 - 2 * p))

    zbase = (take(8), take(8))

    def z_copy(k, rows, target, cols):
        delta = lax.rem(z - target + 8, 8)
        return rdma(t_buf.at[k, rows, pl.ds(pl.multiple_of(cols * 128, 128), 128)],
                    zrecv.at[k, delta], dev_z(target), zbase[k] + delta)

    def chunk_z(k, dz):
        q = m4(zh + dz)
        rows = rows_of(dz)
        second[k, dz, 2].wait_recv()
        second[k, dz, 3].wait_recv()
        t_buf[k, rows] = (s_buf[k, v_own[k], rows].astype(F32) + near2[k, 0, rows].astype(F32)
                          + near2[k, 1, rows].astype(F32)).astype(BF16)
        if dz == 0:
            z_copy(k, rows, 2 * zh + (1 - zl), 1 - zl).start()
        else:
            for l in range(2):
                z_copy(k, rows, 2 * q + l, jnp.int32(l)).start()

    core_z = {}

    def part_pz(dz):
        q = m4(zh + dz)

        def body(j, carry):
            zsend[q, j] = jnp.dot(at_z[q, 1 - c], gs[j], preferred_element_type=F32).astype(BF16)
            return carry

        lax.fori_loop(0, 4, body, 0)
        core_z[dz] = xfer(zsend.at[q], zcrecv.at[q], partner)

    def part_oz(dz):
        q = m4(zh + dz)
        core_z[dz].wait_recv()

        def body(j, carry):
            o_buf[q, j] = (jnp.dot(at_z[q, c], gs[j], preferred_element_type=F32) + zcrecv[q, j].astype(F32)).astype(BF16)
            return carry

        lax.fori_loop(0, 4, body, 0)

    chain = {}
    up, down = dev_z(lax.rem(z + 1, 8)), dev_z(lax.rem(z + 7, 8))

    def z_block(zz):
        return zz // 2, pl.ds(pl.multiple_of(lax.rem(zz, 2) * 128, 128), 128)

    def add_z(zz, j, value):
        q, cols = z_block(zz)
        o_buf[q, j, :, cols] = (o_buf[q, j, :, cols].astype(F32) + value.astype(F32)).astype(BF16)

    def z_far():
        q, cols = z_block(lax.rem(z + 4, 8))
        for p, device in ((0, up), (1, down)):
            chain[4, p, p] = xfer(o_buf.at[q, pl.ds(2 * p, 2), :, cols], zfar.at[p], device)

    def z_step(n, h):
        for p, device in ((0, up), (1, down)):
            zz = lax.rem(z + 8 + (n if p == 0 else -n), 8)
            q, cols = z_block(zz)
            if n == 3:
                if h == p:
                    chain[4, p, p].wait_recv()
                    for j in range(2):
                        add_z(zz, 2 * p + j, zfar[p, j])
            else:
                chain[n + 1, p, h].wait_recv()
                for j in range(2):
                    add_z(zz, 2 * h + j, znear[p, 2 - n, 2 * h + j])
            chain[n, p, h] = xfer(o_buf.at[q, pl.ds(2 * h, 2), :, cols],
                                  znear.at[p, 3 - n, pl.ds(2 * h, 2)], device)

    def z_own(h):
        q, cols = z_block(z)
        for p in range(2):
            chain[1, p, h].wait_recv()
        for j in range(2 * h, 2 * h + 2):
            o_buf[q, j, :, cols] = (o_buf[q, j, :, cols].astype(F32) + znear[0, 2, j].astype(F32)
                                    + znear[1, 2, j].astype(F32)).astype(BF16)
        for d in (2, 1, 3):
            xq = m4(x + d)
            chain["x", d, h] = xfer(o_buf.at[q, pl.ds(2 * h, 2), pl.ds(pl.multiple_of(xq * RC, 16), RC), cols],
                                    xrecv.at[d - 1, pl.ds(2 * h, 2)], dev(dx=d))

    def z_x():
        q, cols = z_block(z)
        for d in (1, 2, 3):
            for h in range(2):
                chain["x", d, h].wait_recv()
        own_x = pl.ds(pl.multiple_of(x * RC, 16), RC)
        for j in range(4):
            total = o_buf[q, j, own_x, cols].astype(F32)
            for d in range(3):
                total = total + xrecv[d, j].astype(F32)
            u_buf[j] = total.astype(BF16)
        for d in (2, 1, 3):
            chain["y", d] = xfer(u_buf.at[m4(y + d)], y3recv.at[d - 1], dev(dy=d))

    part_p(0, 2)
    part_p(1, 2)
    part_pz(2)
    part_p(0, 1)
    far(0)
    far(1)
    part_p(1, 1)
    part_oz(2)
    z_far()
    part_p(0, -1)
    part_pz(-1)
    part_p(1, -1)
    part_pz(1)
    near_free(0, 1)
    near_free(0, -1)
    near_free(1, 1)
    part_oz(-1)
    near_free(1, -1)
    part_oz(1)
    z_step(3, 0)
    near_sum(1, 1)
    z_step(3, 1)
    near_sum(0, -1)
    near_sum(0, 1)
    part_p(1, 0)
    near_sum(1, -1)
    z_step(2, 0)
    part_p(0, 0)
    part_pz(0)
    part_own(1)
    z_step(2, 1)
    part_own(0)
    part_oz(0)
    chunk_sum(1, 2)
    chunk_sum(0, 2)
    z_step(1, 0)
    chunk_sum(1, 1)
    chunk_sum(1, -1)
    z_step(1, 1)
    chunk_mid(1, 2)
    chunk_sum(0, 0)
    chunk_mid(1, 1)
    chunk_sum(0, -1)
    chunk_sum(1, 0)
    chunk_sum(0, 1)
    chunk_mid(1, -1)
    chunk_mid(0, 2)
    z_own(0)
    chunk_mid(0, 0)
    chunk_z(1, 2)
    chunk_mid(0, 1)
    chunk_mid(0, -1)
    chunk_z(1, 1)
    z_own(1)
    chunk_z(1, -1)
    chunk_z(0, 2)
    chunk_mid(1, 0)
    chunk_z(0, 0)
    chunk_z(0, 1)
    chunk_z(0, -1)
    z_x()
    chunk_z(1, 0)

    sums = []
    own_rows = pl.ds(pl.multiple_of(zh * RA, 16), RA)
    for d in (1, 2, 3):
        chain["y", d].wait_recv()
    last = u_buf[y].astype(F32)
    for d in range(3):
        last = last + y3recv[d].astype(F32)
    for k in range(2):
        for d in range(1, 8):
            pltpu.make_async_remote_copy(
                src_ref=zrecv.at[k, 0], dst_ref=zrecv.at[k, d], send_sem=send_sems.at[zbase[k] + d],
                recv_sem=recv_sems.at[zbase[k] + d], device_id=partner, device_id_type=MESH).wait_recv()
        total = t_buf[k, own_rows, pl.ds(pl.multiple_of(zl * 128, 128), 128)].astype(F32)
        for d in range(1, 8):
            total = total + zrecv[k, d].astype(F32)
        sums.append(total)
    total = jnp.concatenate(sums + [last], axis=0).T
    head_cols = pl.ds(pl.multiple_of(512 + y * 128, 128), 128)
    probe_t = wp[zh, x, c, :, head_cols].astype(F32).T
    out[pl.ds(0, 64), :] = total[:64]
    out[pl.ds(64, 64), :] = total[64:] * jnp.where(zl == 0, probe_t[:64], probe_t[64:])

    for cp in sent:
        cp.wait_send()
    for k in range(2):
        for d in range(1, 8):
            pltpu.make_async_remote_copy(
                src_ref=zrecv.at[k, 0], dst_ref=zrecv.at[k, d], send_sem=send_sems.at[zbase[k] + d],
                recv_sem=recv_sems.at[zbase[k] + d], device_id=partner, device_id_type=MESH).wait_send()
    assert count[0] <= NX, count[0]


def on_device(acts, upstream, k_weight, probe, norm_gain, momentum, curvature):
    any_spec = pl.BlockSpec(memory_space=pl.ANY)
    vmem = pl.BlockSpec(memory_space=pltpu.VMEM)
    sums = pl.pallas_call(
        kernel,
        out_shape=jax.ShapeDtypeStruct((128, 224), F32),
        in_specs=[any_spec] * 4 + [vmem],
        out_specs=vmem,
        scratch_shapes=[
            pltpu.VMEM((4, 4, 2, 224, 1024), BF16),
            pltpu.VMEM((TOK, D), BF16),
            pltpu.VMEM((2, 4, 2, 4 * RA, TOK), BF16),
            pltpu.VMEM((TOK, 1024), F32),
            pltpu.VMEM((TOK, 512), BF16),
            pltpu.VMEM((4, TOK, 256), BF16),
            pltpu.VMEM((2, 2, 4, 4 * RA, 256), BF16),
            pltpu.VMEM((2, 4, 4, 4 * RA, 256), BF16),
            pltpu.VMEM((2, 3, 4, 4 * RA, 256), BF16),
            pltpu.VMEM((2, 4, 4 * RA, 256), BF16),
            pltpu.VMEM((2, 2, 4, 4 * RA, 256), BF16),
            pltpu.VMEM((2, 4, 4 * RA, 256), BF16),
            pltpu.VMEM((2, 2, 4 * RA, 128), BF16),
            pltpu.VMEM((2, 2, 4 * RA, 256), BF16),
            pltpu.VMEM((2, 4 * RA, 256), BF16),
            pltpu.VMEM((2, 8, RA, 128), BF16),
            pltpu.VMEM((4, 2, 4 * RC, TOK), BF16),
            pltpu.VMEM((4, 4, 4 * RC, 256), BF16),
            pltpu.VMEM((4, 4, 4 * RC, 256), BF16),
            pltpu.VMEM((4, 4, 4 * RC, 256), BF16),
            pltpu.VMEM((2, 2, 4 * RC, 128), BF16),
            pltpu.VMEM((2, 3, 4, 4 * RC, 128), BF16),
            pltpu.VMEM((3, 4, RC, 128), BF16),
            pltpu.VMEM((4, RC, 128), BF16),
            pltpu.VMEM((3, RC, 128), BF16),
            pltpu.SemaphoreType.DMA((NX,)),
            pltpu.SemaphoreType.DMA((NX,)),
            pltpu.SemaphoreType.DMA((16,)),
        ],
        compiler_params=pltpu.CompilerParams(
            collective_id=0, has_side_effects=True, vmem_limit_bytes=67043328),
    )(acts, upstream, k_weight, probe, norm_gain.reshape(1, 128))
    new_momentum = 0.965 * momentum.T + 0.035 * sums[:64]
    new_curvature = 0.99 * curvature.T + 0.01 * sums[64:]
    update = jnp.clip(new_momentum / jnp.maximum(0.5 * new_curvature, 0.25), -1.0, 1.0)
    return (new_momentum.T, new_curvature.T, update.T)


def solution(mesh):
    return jax.shard_map(
        on_device,
        mesh=mesh,
        in_specs=(
            P(("dp", "fsdp"), None),
            P(("dp", "fsdp"), None),
            P("fsdp", None),
            P("fsdp", None),
            P(),
            P("fsdp", "dp"),
            P("fsdp", "dp"),
        ),
        out_specs=(P("fsdp", "dp"), P("fsdp", "dp"), P("fsdp", "dp")),
        check_vma=False,
    )
```
